32 devices in a mesh: dp: 8 (over z, x), seq: 4 (over y, core).
Axes of the slice: x: 2, y: 2, z: 4, core: 2. Of those that a mesh axis runs over, the one named last changes fastest.
Arguments:
- tokens: bfloat16 [2, 8, 1024, 2048], P(None, 'dp', 'seq'), may hold values from -6 to 6
- lengths: int32 [2, 8], P(None, 'dp'), may hold values from 256 to 1024, as said below
- cotangent: bfloat16 [2, 8, 1024, 2048], P(None, 'dp', 'seq'), may hold values from -6 to 6
- norm_gain: bfloat16 [2048], P(('dp', 'seq')), may hold values from 0.099609375 to 1.8984375
- in_weight: bfloat16 [2048, 8192], P(('dp', 'seq')), may hold values from -0.125 to 0.125
- conv_weight: bfloat16 [4, 4096], P(None, ('dp', 'seq')), may hold values from -3 to 3
- conv_bias: bfloat16 [4096], P(('dp', 'seq')), may hold values from -3 to 3
- x_weight: bfloat16 [4096, 160], P(('dp', 'seq')), may hold values from -0.09375 to 0.09375
- dt_weight: bfloat16 [128, 4096], P(None, ('dp', 'seq')), may hold values from -0.5 to 0.5
- dt_bias: bfloat16 [4096], P(('dp', 'seq')), may hold values from -8 to -2
- a_log: bfloat16 [16, 4096], P(None, ('dp', 'seq')), may hold values from -2 to 2.765625
- skip_d: bfloat16 [4096], P(('dp', 'seq')), may hold values from 0.5 to 2
- out_weight: bfloat16 [4096, 2048], P(('dp', 'seq')), may hold values from -0.25 to 0.25
Outputs:
- block_out: bfloat16 [2, 8, 1024, 2048], P(None, 'dp', 'seq')
- input_grad: bfloat16 [2, 8, 1024, 2048], P(None, 'dp', 'seq')
- grad_norm_gain: float32 [2048], P(('dp', 'seq'))
- grad_in_weight: float32 [2048, 8192], P(('dp', 'seq'))
- grad_conv_weight: float32 [4, 4096], P(None, ('dp', 'seq'))
- grad_conv_bias: float32 [4096], P(('dp', 'seq'))
- grad_x_weight: float32 [4096, 160], P(('dp', 'seq'))
- grad_dt_weight: float32 [128, 4096], P(None, ('dp', 'seq'))
- grad_dt_bias: float32 [4096], P(('dp', 'seq'))
- grad_a_log: float32 [16, 4096], P(None, ('dp', 'seq'))
- grad_skip_d: float32 [4096], P(('dp', 'seq'))
- grad_out_weight: float32 [4096, 2048], P(('dp', 'seq'))
The draws below stay inside these ranges and needn't reach their ends.
Inputs may be any that keep to these rules, and one draw needn't show every extreme that they name: `lengths`: the number of leading positions of each slot that hold tokens; later positions are padding.
All inputs are finite; a program needn't handle non-finite values.
Results may differ from the reference program's by a relative error of at most 0.012.
Values may be sent and summed in bfloat16 or wider, within the bound.
No kernel may reach another device: no remote copies, remote signals or barrier semaphores. Data moves between devices by JAX's collectives and lax.ppermute only.
A program may use at most 320 MiB of HBM per device.

```python
import jax
import jax.numpy as jnp
from jax import lax

D = 2048
INNER = 4096
RANK = 128
STATE = 16
KCONV = 4
BLOCK = 16
MICRO = 2
SLOTS = 8
SLOT = 1024


def draw_lengths(key, part):
    base = jax.random.randint(key, (MICRO * SLOTS,), SLOT // 4, SLOT + 1)
    order = jax.random.permutation(jax.random.fold_in(key, 7), MICRO * SLOTS)
    base = base.at[order[0]].set(SLOT)
    base = base.at[order[1]].set(SLOT // 4)
    return base.reshape(MICRO, SLOTS).astype(jnp.int32)


def shard_levels(stream_key, dims, cuts, low, top_value):
    level = 1.0
    for axis_at, shards_of in cuts:
        heights = jax.random.uniform(jax.random.fold_in(jax.random.fold_in(stream_key, 6), axis_at), (shards_of,), jnp.float32, low / len(cuts), top_value / len(cuts))
        level = level * jnp.repeat(jnp.exp(heights), dims[axis_at] // shards_of).reshape((-1,) + (1,) * (len(dims) - 1 - axis_at))
    return level


def scatter_about(rng, dims, width, most, shards=(), kind=jnp.bfloat16):
    drawn = jax.random.normal(rng, dims, jnp.float32) * width
    if len(shards) > 0:
        drawn = shard_levels(rng, dims, shards, -0.22, 0.18) * drawn
    return jnp.clip(drawn, min=-most, max=most).astype(kind)


def setup_inputs(seed: int = 0) -> dict:
    seeds = jax.random.split(jax.random.key(seed), 14)
    return {
        "tokens": scatter_about(seeds[0], (MICRO, SLOTS, SLOT, D), 1.0, 6.0, ((1, 8), (2, 4))),
        "lengths": draw_lengths(jax.random.fold_in(seeds[13], 71), 0),
        "cotangent": scatter_about(seeds[2], (MICRO, SLOTS, SLOT, D), 1.0, 6.0, ((1, 8), (2, 4))),
        "norm_gain": jnp.clip(1.0 + 0.18 * jax.random.normal(seeds[3], (D,), jnp.float32), 0.099609375, 1.8984375).astype(jnp.bfloat16),
        "in_weight": scatter_about(seeds[4], (D, 2 * INNER), D ** -0.5, 0.125, ((0, 32),)),
        "conv_weight": scatter_about(seeds[5], (KCONV, INNER), KCONV ** -0.5, 3.0, ((1, 32),)),
        "conv_bias": scatter_about(seeds[6], (INNER,), 0.5, 3.0, ((0, 32),)),
        "x_weight": scatter_about(seeds[7], (INNER, RANK + 2 * STATE), INNER ** -0.5, 0.09375, ((0, 32),)),
        "dt_weight": scatter_about(seeds[8], (RANK, INNER), RANK ** -0.5, 0.5, ((1, 32),)),
        "dt_bias": jnp.clip(-8.0 + 6.0 * jax.random.uniform(seeds[9], (INNER,), jnp.float32) ** shard_levels(seeds[9], (INNER,), ((0, 32),), -0.2, 0.2), -8.0, -2.0).astype(jnp.bfloat16),
        "a_log": jnp.clip(-2.0 + 4.765625 * jax.random.uniform(seeds[10], (STATE, INNER), jnp.float32) ** shard_levels(seeds[10], (STATE, INNER), ((1, 32),), -0.2, 0.2), -2.0, 2.765625).astype(jnp.bfloat16),
        "skip_d": jnp.clip(0.5 + 1.5 * jax.random.uniform(seeds[11], (INNER,), jnp.float32) ** shard_levels(seeds[11], (INNER,), ((0, 32),), -0.2, 0.2), 0.5, 2.0).astype(jnp.bfloat16),
        "out_weight": scatter_about(seeds[12], (INNER, D), (INNER // 8) ** -0.5, 0.25, ((0, 32),)),
    }


@jax.custom_vjp
def low(v):
    return lax.optimization_barrier(v.astype(jnp.bfloat16)).astype(jnp.float32)

@jax.custom_vjp
def low_back(v):
    return v

def low_keep(v):
    return (low(v), None)

def low_pass(kept, grad):
    return (grad,)

def back_keep(v):
    return (v, None)

def back_low(kept, grad):
    return (low(grad),)
low.defvjp(low_keep, low_pass)
low_back.defvjp(back_keep, back_low)

def product(left, right):
    return jnp.dot(left, right, precision=lax.Precision.HIGHEST, preferred_element_type=jnp.float32)

def selective(step_size, b_in, c_out, conv_out, decay_rate):

    def token(state, pieces):
        steps, b_row, c_row, x_row = pieces
        factor = jnp.exp(steps[None, :] * decay_rate)
        state = factor * state + b_row[:, None] * (steps * x_row)[None, :]
        return (state, lax.optimization_barrier(jnp.sum(c_row[:, None] * state, axis=0)))

    def block(state, pieces):
        return lax.scan(token, state, pieces)
    shaped = tuple((value.reshape((SLOT // BLOCK, BLOCK) + value.shape[1:]) for value in (step_size, b_in, c_out, conv_out)))
    initial = jnp.zeros((STATE, INNER), jnp.float32)
    final, outputs = lax.scan(jax.checkpoint(block), initial, shaped)
    return outputs.reshape(SLOT, INNER)

def forward(inputs, params, valid):
    gain, input_projection, w_conv, b_conv, w_x, w_dt, b_dt, a_log, skip, output_projection = params
    scale = lax.rsqrt(lax.optimization_barrier(jnp.mean(inputs * inputs, axis=-1, keepdims=True)) + 1e-05)
    normalized_input = low(inputs * scale * gain)
    mixer_output = low_back(product(normalized_input, input_projection))
    branch_in = low(mixer_output[:, :INNER])
    gate_pre = mixer_output[:, INNER:]
    padded = jnp.concatenate([jnp.zeros((KCONV - 1, INNER), jnp.float32), branch_in], axis=0)
    conv_pre = b_conv + sum((w_conv[k] * padded[k:k + SLOT] for k in range(KCONV)))
    conv_out = low(jax.nn.silu(conv_pre))
    proj = low_back(product(conv_out, w_x))
    step_low = low(proj[:, :RANK])
    b_in = proj[:, RANK:RANK + STATE]
    c_out = proj[:, RANK + STATE:]
    step_pre = low_back(product(step_low, w_dt)) + b_dt
    step_size = jax.nn.softplus(step_pre)
    decay_rate = -jnp.exp(a_log)
    scan_out = selective(step_size, b_in, c_out, conv_out, decay_rate) + skip * conv_out
    gated_output = low(scan_out * jax.nn.silu(gate_pre))
    residual_branch = low_back(product(gated_output, output_projection))
    return valid[:, None] * (inputs + residual_branch)

def reference(tokens, lengths, cotangent, norm_gain, in_weight, conv_weight, conv_bias, x_weight, dt_weight, dt_bias, a_log, skip_d, out_weight):
    params = tuple((weight.astype(jnp.float32) for weight in (norm_gain, in_weight, conv_weight, conv_bias, x_weight, dt_weight, dt_bias, a_log, skip_d, out_weight)))
    inputs_all = tokens.reshape(MICRO * SLOTS, SLOT, D).astype(jnp.float32)
    cots_all = cotangent.reshape(MICRO * SLOTS, SLOT, D).astype(jnp.float32)
    lengths_all = lengths.reshape(MICRO * SLOTS).astype(jnp.int32)

    def one_slot(totals, pieces):
        inputs, cots, length = pieces
        valid = (jnp.arange(SLOT, dtype=jnp.int32) < length).astype(jnp.float32)
        result, pull = jax.vjp(lambda first, second: forward(first, second, valid), inputs, params)
        grad_inputs, grad_params = pull(cots)
        totals = jax.tree.map(lambda total, grad: total + grad, totals, grad_params)
        return (totals, (result.astype(jnp.bfloat16), grad_inputs.astype(jnp.bfloat16)))
    zeros = tuple((jnp.zeros(weight.shape, jnp.float32) for weight in params))
    totals, (results, input_grads) = lax.scan(one_slot, zeros, (inputs_all, cots_all, lengths_all))
    shape = (MICRO, SLOTS, SLOT, D)
    return (results.reshape(shape), input_grads.reshape(shape), totals[0], totals[1], totals[2], totals[3], totals[4], totals[5], totals[6], totals[7], totals[8], totals[9])
```

```python
import jax
import jax.numpy as jnp
from jax import lax
from jax.experimental import pallas as pl
from jax.experimental.pallas import tpu as pltpu
from jax.sharding import PartitionSpec as P

F32 = jnp.float32
BF16 = jnp.bfloat16
LOG2E = 1.4426950408889634
CHUNK = 128
KCONV = 4
EPSILON = 1e-05


def softplus(v):
    return jnp.maximum(v, 0.0) + jnp.log1p(jnp.exp(-jnp.abs(v)))


def expand_states(bc_ref, spread):
    rows, length = bc_ref.shape
    for t in range(length):
        spread[t * rows:(t + 1) * rows, :] = jnp.broadcast_to(bc_ref[:, t:t + 1], (rows, 128))


def lanes_of(value, width):
    return jnp.concatenate([value] * (width // 128), axis=1) if width > 128 else value


def fold(value, width):
    total = value[:, 0:128]
    for at in range(128, width, 128):
        total = total + value[:, at:at + 128]
    return total


def scan_forward_kernel(order, proj_ref, x_ref, dtw_ref, dtb_ref, alog_ref, skip_ref, held_ref,
                        y_ref, start_ref, state, steps, drive, spread, part, ysum, *, width):
    length, inner = x_ref.shape

    @pl.when(pl.program_id(0) == 0)
    def _():
        state[...] = jnp.zeros_like(state)

    start_ref[0] = state[...]
    xs = x_ref[...].astype(F32)
    pre = jnp.dot(proj_ref[0:length, :].astype(BF16), dtw_ref[...], preferred_element_type=F32) + dtb_ref[...]
    step = softplus(pre)
    steps[...] = step
    drive[...] = step * xs
    expand_states(proj_ref.at[length:, :], spread)
    blocks = width // 128

    def group(g, _):
        lanes = pl.ds(pl.multiple_of(g * width, width), width)
        rate = -jnp.exp(alog_ref[:, lanes].astype(F32)) * LOG2E

        def eight(i, h):
            base = pl.multiple_of(i * 8, 8)
            for r in range(8):
                st = steps[pl.ds(base + r, 1), lanes]
                dr = drive[pl.ds(base + r, 1), lanes]
                at = (base + r) * 32
                b = lanes_of(spread[pl.ds(pl.multiple_of(at, 32), 16), :], width)
                c = lanes_of(spread[pl.ds(pl.multiple_of(at + 16, 16), 16), :], width)
                h = jnp.exp2(st * rate) * h + b * dr
                p = c * h
                p = p[0:8] + p[8:16]
                for j in range(blocks):
                    part[j, r * 8:(r + 1) * 8, :] = p[:, j * 128:(j + 1) * 128]
            for j in range(blocks):
                total = part[j, pl.ds(0, 8, stride=8), :]
                for k in range(1, 8):
                    total = total + part[j, pl.ds(k, 8, stride=8), :]
                ysum[pl.ds(base, 8), pl.ds(pl.multiple_of(g * width + j * 128, 128), 128)] = total
            return h

        state[:, lanes] = lax.fori_loop(0, length // 8, eight, state[:, lanes])
        return 0

    lax.fori_loop(0, inner // width, group, 0)
    y_ref[...] = (ysum[...] + skip_ref[...] * xs).astype(y_ref.dtype)


def spec_nat(length, cols):
    return pl.BlockSpec((length, cols), lambda i, order: (i, 0))


def whole_spec(shape):
    return pl.BlockSpec(shape, lambda i, order: (0,) * len(shape))


def placed(per_piece, count, reverse=False, base=0):
    def index(i, order):
        at = count - 1 - i if reverse else i
        return (order[at // per_piece] * per_piece + at % per_piece + base, 0)
    return index


def scan_forward(order, proj, x, dtw, dtb, alog, skip, micro, micros, held, width=512):
    length, inner = x.shape
    count = length // CHUNK
    states = alog.shape[0]
    rank = dtw.shape[0]
    per_piece = count // order.shape[0]
    width = min(width, inner)
    first = held is None
    return pl.pallas_call(
        lambda *refs: scan_forward_kernel(*refs, width=width),
        grid_spec=pltpu.PrefetchScalarGridSpec(
            num_scalar_prefetch=1,
            grid=(count,),
            in_specs=[
                spec_nat(CHUNK + 2 * states, rank), spec_nat(CHUNK, inner),
                whole_spec((rank, inner)), whole_spec((1, inner)), whole_spec((states, inner)), whole_spec((1, inner)),
                pl.BlockSpec(memory_space=pl.ANY),
            ],
            out_specs=[
                pl.BlockSpec((CHUNK, inner), placed(per_piece, count, False, micro * count)),
                pl.BlockSpec((1, states, inner), lambda i, order: (i, 0, 0)),
            ],
            scratch_shapes=[
                pltpu.VMEM((states, inner), F32),
                pltpu.VMEM((CHUNK, inner), F32),
                pltpu.VMEM((CHUNK, inner), F32),
                pltpu.VMEM((CHUNK * 2 * states, 128), F32),
                pltpu.VMEM((width // 128, 64, 128), F32),
                pltpu.VMEM((CHUNK, inner), F32),
            ],
        ),
        out_shape=[
            jax.ShapeDtypeStruct((micros * length, inner), BF16),
            jax.ShapeDtypeStruct((count, states, inner), F32),
        ],
        input_output_aliases={} if first else {7: 0},
        name="scan_forward",
    )(order, proj, x, dtw, dtb, alog, skip, dtb if first else held)


def scan_backward_kernel(order, proj_ref, x_ref, sg_ref, start_ref, dtw_ref, dtb_ref, alog_ref, skip_ref,
                         pg_ref, xg_ref, gdtw_ref, gdtb_ref, galog_ref, gskip_ref,
                         adjoint, steps, drive, grads, spread, hist, fac, bsum, csum, part, part2, lamb, stepg, *, width):
    length, inner = x_ref.shape
    first = pl.program_id(0) == 0

    @pl.when(first)
    def _():
        adjoint[...] = jnp.zeros_like(adjoint)
        gdtw_ref[...] = jnp.zeros_like(gdtw_ref)
        gdtb_ref[...] = jnp.zeros_like(gdtb_ref)
        galog_ref[...] = jnp.zeros_like(galog_ref)
        gskip_ref[...] = jnp.zeros_like(gskip_ref)

    xs = x_ref[...].astype(F32)
    low = proj_ref[0:length, :].astype(BF16)
    pre = jnp.dot(low, dtw_ref[...], preferred_element_type=F32) + dtb_ref[...]
    step = softplus(pre)
    steps[...] = step
    drive[...] = step * xs
    grads[...] = sg_ref[...].astype(F32)
    expand_states(proj_ref.at[length:, :], spread)
    bsum[...] = jnp.zeros_like(bsum)
    csum[...] = jnp.zeros_like(csum)
    blocks = width // 128

    def group(g, _):
        lanes = pl.ds(pl.multiple_of(g * width, width), width)
        decay = -jnp.exp(alog_ref[:, lanes].astype(F32))
        rate = decay * LOG2E

        def again(i, h):
            base = pl.multiple_of(i * 8, 8)
            for r in range(8):
                st = steps[pl.ds(base + r, 1), lanes]
                dr = drive[pl.ds(base + r, 1), lanes]
                sg = grads[pl.ds(base + r, 1), lanes]
                b = lanes_of(spread[pl.ds(pl.multiple_of((base + r) * 32, 32), 16), :], width)
                row = pl.ds(pl.multiple_of((base + r) * 16, 16), 16)
                hist[row, :] = h
                a = jnp.exp2(st * rate)
                fac[row, :] = a
                h = a * h + b * dr
                csum[row, :] += fold(sg * h, width)
            return h

        lax.fori_loop(0, length // 8, again, start_ref[0, :, lanes])

        def back(i, carry):
            adj, dsum = carry
            base = pl.multiple_of(length - 8 - i * 8, 8)
            for r in reversed(range(8)):
                st = steps[pl.ds(base + r, 1), lanes]
                dr = drive[pl.ds(base + r, 1), lanes]
                sg = grads[pl.ds(base + r, 1), lanes]
                at = (base + r) * 32
                b = lanes_of(spread[pl.ds(pl.multiple_of(at, 32), 16), :], width)
                c = lanes_of(spread[pl.ds(pl.multiple_of(at + 16, 16), 16), :], width)
                row = pl.ds(pl.multiple_of((base + r) * 16, 16), 16)
                lam = adj + c * sg
                bsum[row, :] += fold(lam * dr, width)
                adj = fac[row, :] * lam
                w = adj * hist[row, :]
                dsum = dsum + w * st
                p = lam * b
                p = p[0:8] + p[8:16]
                q = w * decay
                q = q[0:8] + q[8:16]
                for j in range(blocks):
                    part[j, r * 8:(r + 1) * 8, :] = p[:, j * 128:(j + 1) * 128]
                    part2[j, r * 8:(r + 1) * 8, :] = q[:, j * 128:(j + 1) * 128]
            for j in range(blocks):
                total = part[j, pl.ds(0, 8, stride=8), :]
                total2 = part2[j, pl.ds(0, 8, stride=8), :]
                for k in range(1, 8):
                    total = total + part[j, pl.ds(k, 8, stride=8), :]
                    total2 = total2 + part2[j, pl.ds(k, 8, stride=8), :]
                where = pl.ds(pl.multiple_of(g * width + j * 128, 128), 128)
                lamb[pl.ds(base, 8), where] = total
                stepg[pl.ds(base, 8), where] = total2
            return adj, dsum

        adj, dsum = lax.fori_loop(0, length // 8, back, (adjoint[:, lanes], jnp.zeros((16, width), F32)))
        adjoint[:, lanes] = adj
        galog_ref[:, lanes] += dsum * decay
        return 0

    lax.fori_loop(0, inner // width, group, 0)
    xs = x_ref[...].astype(F32)
    sg = grads[...]
    lam_b = lamb[...]
    low = proj_ref[0:length, :].astype(BF16)
    pre = jnp.dot(low, dtw_ref[...], preferred_element_type=F32) + dtb_ref[...]
    sig = 1.0 / (1.0 + jnp.exp(-pre))
    pre_grad = (stepg[...] + xs * lam_b) * sig
    gdtb_ref[...] += jnp.sum(pre_grad, axis=0, keepdims=True)
    gskip_ref[...] += jnp.sum(sg * xs, axis=0, keepdims=True)
    xg_ref[...] = (steps[...] * lam_b + skip_ref[...] * sg).astype(xg_ref.dtype)
    pre_low = pre_grad.astype(BF16)
    gdtw_ref[...] += lax.dot_general(low, pre_low, (((0,), (0,)), ((), ())), preferred_element_type=F32)
    pg_ref[0:length, :] = lax.dot_general(pre_low, dtw_ref[...], (((1,), (1,)), ((), ())), preferred_element_type=F32)
    states = adjoint.shape[0]
    rows = length * states
    ones = jnp.ones((128, 128), F32)
    token = lax.broadcasted_iota(jnp.int32, (rows, length), 0) // states
    here = token == lax.broadcasted_iota(jnp.int32, (rows, length), 1)
    state = lax.broadcasted_iota(jnp.int32, (states, rows), 1) % states
    pick = (state == lax.broadcasted_iota(jnp.int32, (states, rows), 0)).astype(F32)
    for at, sums in ((length, bsum), (length + states, csum)):
        total = jnp.dot(sums[...], ones, preferred_element_type=F32)
        pg_ref[at:at + states, :] = jnp.dot(pick, jnp.where(here, total, 0.0), preferred_element_type=F32)


def scan_backward(order, proj, x, sg, starts, dtw, dtb, alog, skip, micro, width=512):
    length, inner = x.shape
    count = length // CHUNK
    states = alog.shape[0]
    rank = dtw.shape[0]
    per_piece = count // order.shape[0]
    width = min(width, inner)
    rev = lambda cols: pl.BlockSpec((CHUNK, cols), lambda i, order: (count - 1 - i, 0))
    return pl.pallas_call(
        lambda *refs: scan_backward_kernel(*refs, width=width),
        grid_spec=pltpu.PrefetchScalarGridSpec(
            num_scalar_prefetch=1,
            grid=(count,),
            in_specs=[
                pl.BlockSpec((CHUNK + 2 * states, rank), lambda i, order: (count - 1 - i, 0)), rev(inner),
                pl.BlockSpec((CHUNK, inner), placed(per_piece, count, True, micro * count)),
                pl.BlockSpec((1, states, inner), lambda i, order: (count - 1 - i, 0, 0)),
                whole_spec((rank, inner)), whole_spec((1, inner)), whole_spec((states, inner)), whole_spec((1, inner)),
            ],
            out_specs=[
                pl.BlockSpec((CHUNK + 2 * states, rank), lambda i, order: (count - 1 - i, 0)),
                rev(inner),
                whole_spec((rank, inner)), whole_spec((1, inner)), whole_spec((states, inner)), whole_spec((1, inner)),
            ],
            scratch_shapes=[
                pltpu.VMEM((states, inner), F32),
                pltpu.VMEM((CHUNK, inner), F32),
                pltpu.VMEM((CHUNK, inner), F32),
                pltpu.VMEM((CHUNK, inner), F32),
                pltpu.VMEM((CHUNK * 2 * states, 128), F32),
                pltpu.VMEM((CHUNK * states, width), F32),
                pltpu.VMEM((CHUNK * states, width), F32),
                pltpu.VMEM((CHUNK * states, 128), F32),
                pltpu.VMEM((CHUNK * states, 128), F32),
                pltpu.VMEM((width // 128, 64, 128), F32),
                pltpu.VMEM((width // 128, 64, 128), F32),
                pltpu.VMEM((CHUNK, inner), F32),
                pltpu.VMEM((CHUNK, inner), F32),
            ],
        ),
        out_shape=[
            jax.ShapeDtypeStruct((count * (CHUNK + 2 * states), rank), F32),
            jax.ShapeDtypeStruct((length, inner), BF16),
            jax.ShapeDtypeStruct((rank, inner), F32),
            jax.ShapeDtypeStruct((1, inner), F32),
            jax.ShapeDtypeStruct((states, inner), F32),
            jax.ShapeDtypeStruct((1, inner), F32),
        ],
        name="scan_backward",
    )(order, proj, x, sg, starts, dtw, dtb, alog, skip)


def conv_forward_kernel(order, *refs, peers):
    pieces = refs[:peers]
    gain_ref, wb_ref, cw_ref, cb_ref, xw_ref, held_ref, normed_ref, branch_ref, x_ref, proj_ref, pad = refs[peers:]
    length, inner = x_ref.shape
    at = pl.program_id(0)

    @pl.when(at == 0)
    def _():
        pad[0:8, :] = jnp.zeros((8, inner), F32)

    for p in range(peers):
        @pl.when(order[at] == p)
        def _():
            tokens = pieces[p][...].astype(F32)
            scale = lax.rsqrt(jnp.mean(tokens * tokens, axis=-1, keepdims=True) + EPSILON)
            normed_ref[...] = (tokens * scale * gain_ref[...]).astype(BF16)

    groups = wb_ref.shape[0]
    deep = normed_ref.shape[1] // groups
    branch = sum(jnp.dot(normed_ref[:, d * deep:(d + 1) * deep], wb_ref[d, 0:deep, :], preferred_element_type=F32)
                 for d in range(groups)).astype(BF16)
    branch_ref[...] = branch
    pad[8:8 + length, :] = branch.astype(F32)
    pre = cb_ref[...] + sum(cw_ref[k:k + 1, :] * pad[5 + k:5 + k + length, :] for k in range(KCONV))
    x = (pre / (1.0 + jnp.exp(-pre))).astype(BF16)
    x_ref[...] = x
    rank = proj_ref.shape[1]
    low = lax.dot_general(x, xw_ref[0:rank, :], (((1,), (1,)), ((), ())), preferred_element_type=F32)
    maps = lax.dot_general(xw_ref[rank:, :], x, (((1,), (1,)), ((), ())), preferred_element_type=F32)
    rows = CHUNK + maps.shape[0]
    for at in range(length // CHUNK):
        proj_ref[at * rows:at * rows + CHUNK, :] = low[at * CHUNK:(at + 1) * CHUNK, :]
        proj_ref[at * rows + CHUNK:(at + 1) * rows, :] = maps[:, at * CHUNK:(at + 1) * CHUNK]
    pad[0:8, :] = pad[length:length + 8, :]


def conv_forward(order, pieces, gain, wb, cw, cb, xw, rank, micro, micros, held):
    peers = len(pieces)
    tokens, width = pieces[0].shape
    inner = wb.shape[2]
    cols = xw.shape[0]
    rows = tokens // CHUNK * (CHUNK + cols - rank)
    first = held is None
    return pl.pallas_call(
        lambda *refs: conv_forward_kernel(*refs, peers=peers),
        grid_spec=pltpu.PrefetchScalarGridSpec(
            num_scalar_prefetch=1,
            grid=(peers,),
            in_specs=[whole_spec((tokens, width))] * peers + [
                whole_spec((1, width)),
                whole_spec(wb.shape), whole_spec((KCONV, inner)), whole_spec((1, inner)), whole_spec((cols, inner)),
                pl.BlockSpec(memory_space=pl.ANY),
            ],
            out_specs=[
                pl.BlockSpec((tokens, width), placed(1, peers, False, micro * peers)),
                spec_nat(tokens, inner), spec_nat(tokens, inner), spec_nat(rows, rank),
            ],
            scratch_shapes=[pltpu.VMEM((tokens + 8, inner), F32)],
        ),
        out_shape=[
            jax.ShapeDtypeStruct((micros * peers * tokens, width), BF16),
            jax.ShapeDtypeStruct((peers * tokens, inner), BF16),
            jax.ShapeDtypeStruct((peers * tokens, inner), BF16),
            jax.ShapeDtypeStruct((peers * rows, rank), F32),
        ],
        input_output_aliases={} if first else {peers + 6: 0},
        name="conv_forward",
    )(order, *pieces, gain, wb, cw, cb, xw, gain if first else held)


def conv_backward_kernel(order, pg_ref, xg_ref, branch_ref, prev_ref, x_ref, cw_ref, cb_ref, xw_ref, held_ref,
                         mixed_ref, gxw_ref, gcb_ref, gcw_ref, pad, ahead):
    length, inner = x_ref.shape

    @pl.when(pl.program_id(0) == 0)
    def _():
        ahead[length:length + 8, :] = jnp.zeros((8, inner), F32)
        gxw_ref[...] = jnp.zeros_like(gxw_ref)
        gcb_ref[...] = jnp.zeros_like(gcb_ref)
        gcw_ref[...] = jnp.zeros_like(gcw_ref)

    earliest = pl.program_id(0) == pl.num_programs(0) - 1
    pad[0:8, :] = jnp.where(earliest, 0.0, prev_ref[...].astype(F32)[8:16, :])
    pad[8:8 + length, :] = branch_ref[...].astype(F32)
    pre = cb_ref[...] + sum(cw_ref[k:k + 1, :] * pad[5 + k:5 + k + length, :] for k in range(KCONV))
    sig = 1.0 / (1.0 + jnp.exp(-pre))
    rank = pg_ref.shape[1]
    rows = CHUNK + xw_ref.shape[0] - rank
    low, maps = [], []
    for at in range(length // CHUNK):
        low.append(pg_ref[at * rows:at * rows + CHUNK, :].astype(BF16))
        maps.append(pg_ref[at * rows + CHUNK:(at + 1) * rows, :].astype(BF16))
    low, maps = jnp.concatenate(low, axis=0), jnp.concatenate(maps, axis=1)
    grad = (jnp.dot(low, xw_ref[0:rank, :], preferred_element_type=F32)
            + lax.dot_general(maps, xw_ref[rank:, :], (((0,), (0,)), ((), ())), preferred_element_type=F32)
            + xg_ref[...].astype(F32))
    grad = grad * (sig * (1.0 + pre * (1.0 - sig)))
    ahead[0:length, :] = grad
    gcb_ref[...] += jnp.sum(grad, axis=0, keepdims=True)
    for k in range(KCONV):
        gcw_ref[k:k + 1, :] += jnp.sum(grad * pad[5 + k:5 + k + length, :], axis=0, keepdims=True)
    mixed = sum(cw_ref[k:k + 1, :] * ahead[3 - k:3 - k + length, :] for k in range(KCONV))
    mixed_ref[...] = mixed.astype(BF16)
    gxw_ref[0:rank, :] += lax.dot_general(low, x_ref[...], (((0,), (0,)), ((), ())), preferred_element_type=F32)
    gxw_ref[rank:, :] += jnp.dot(maps, x_ref[...], preferred_element_type=F32)
    ahead[length:length + 8, :] = ahead[0:8, :]


def conv_backward(order, pg, xg, branch, x, cw, cb, xw, micro, micros, held):
    length, inner = x.shape
    tokens = length // order.shape[0]
    count = length // tokens
    cols = xw.shape[0]
    first = held is None
    rank = pg.shape[1]
    rows = pg.shape[0] // count
    rev = lambda width: pl.BlockSpec((tokens, width), lambda i, order: (count - 1 - i, 0))
    return pl.pallas_call(
        conv_backward_kernel,
        grid_spec=pltpu.PrefetchScalarGridSpec(
            num_scalar_prefetch=1,
            grid=(count,),
            in_specs=[
                pl.BlockSpec((rows, rank), lambda i, order: (count - 1 - i, 0)), rev(inner), rev(inner),
                pl.BlockSpec((16, inner), lambda i, order: (jnp.maximum((count - 1 - i) * (tokens // 16) - 1, 0), 0)),
                rev(inner),
                whole_spec((KCONV, inner)), whole_spec((1, inner)), whole_spec((cols, inner)),
                pl.BlockSpec(memory_space=pl.ANY),
            ],
            out_specs=[
                pl.BlockSpec((tokens, inner), placed(1, count, True, micro * count)),
                whole_spec((cols, inner)), whole_spec((1, inner)), whole_spec((KCONV, inner)),
            ],
            scratch_shapes=[pltpu.VMEM((tokens + 8, inner), F32), pltpu.VMEM((tokens + 8, inner), F32)],
        ),
        out_shape=[
            jax.ShapeDtypeStruct((micros * length, inner), BF16),
            jax.ShapeDtypeStruct((cols, inner), F32),
            jax.ShapeDtypeStruct((1, inner), F32),
            jax.ShapeDtypeStruct((KCONV, inner), F32),
        ],
        input_output_aliases={} if first else {9: 0},
        name="conv_backward",
    )(order, pg, xg, branch, branch, x, cw, cb, xw, cb if first else held)


def partner(value, step):
    peers = lax.axis_size("seq")
    return lax.ppermute(value, "seq", [(i, i ^ step) for i in range(peers)])


def halvings():
    step = lax.axis_size("seq") // 2
    while step >= 1:
        yield step
        step //= 2


def reversed_bits(value, peers):
    out = value * 0
    step = 1
    while step < peers:
        out = out * 2 + (value // step) % 2
        step *= 2
    return out


def sum_to_piece(partial, axis):
    for step in reversed(list(halvings())):
        kept, given = jnp.split(partial, 2, axis=axis)
        partial = kept.astype(F32) + partner(given, step).astype(F32)
        if step < lax.axis_size("seq") // 2:
            partial = partial.astype(BF16)
    return partial


def sum_over_pieces(value):
    for step in reversed(list(halvings())[:-1]):
        value = value.astype(F32) + partner(value, step).astype(F32)
        value = value if step == lax.axis_size("seq") // 2 else value.astype(BF16)
    return value


def sum_to_owner(whole):
    ranks = lax.axis_size("dp")
    me = lax.axis_index("dp")
    share = whole.shape[1] // ranks
    parts = jnp.stack([lax.dynamic_slice_in_dim(whole, (me ^ r) * share, share, 1) for r in range(ranks)]).astype(F32)
    step = 1
    while parts.shape[0] > 1:
        parts = parts.reshape((parts.shape[0] // 2, 2) + parts.shape[1:])
        given = parts[:, 1].astype(BF16)
        other = lax.ppermute(given, "dp", [(i, i ^ step) for i in range(ranks)])
        parts = parts[:, 0] + other.astype(F32)
        step *= 2
    return parts[0]


def dot(left, right, dims, kind=F32):
    return lax.dot_general(left, right, (dims, ((), ())), preferred_element_type=kind)


def body(tokens, lengths, cotangent, norm_gain, in_weight, conv_weight, conv_bias, x_weight, dt_weight,
         dt_bias, a_log, skip_d, out_weight):
    micros, slots, piece, width = tokens.shape
    peers, groups = lax.axis_size("seq"), lax.axis_size("dp")
    me = lax.axis_index("seq")
    share = conv_bias.shape[0]
    inner = share * groups
    rows = in_weight.shape[0]
    rank = dt_weight.shape[0]
    states = a_log.shape[0]
    cols = x_weight.shape[1]
    length = piece * peers
    order = reversed_bits(jnp.arange(peers, dtype=jnp.int32) ^ me, peers)
    tokens, cotangent = tokens[:, 0], cotangent[:, 0]

    gain_part = norm_gain
    for step in halvings():
        gain_part = jnp.concatenate([gain_part, partner(gain_part, step)])
    gain_part = gain_part.reshape(peers, rows)
    gain_part = jnp.concatenate([lax.dynamic_slice_in_dim(gain_part, order[q], 1) for q in range(peers)])
    gain_rows = peers * rows // share
    small = jnp.concatenate([
        a_log, conv_weight, conv_bias[None], dt_bias[None], skip_d[None], gain_part.reshape(gain_rows, share),
        jnp.zeros((states - KCONV - 3 - gain_rows, share), BF16), dt_weight, x_weight.T], axis=0)
    packed = small.shape[0]

    def mine(half):
        own = half.reshape(rows, groups, peers, share).transpose(2, 0, 1, 3).reshape(peers * rows, inner)
        return lax.all_to_all(own, "seq", split_axis=0, concat_axis=0, tiled=True)

    first = jnp.concatenate([mine(in_weight[:, :inner * peers]), small.reshape(-1, inner)], axis=0)
    first = lax.all_gather(first, "dp", axis=0, tiled=False)
    pieces = [[tokens[m]] for m in range(micros)]
    for step in halvings():
        for m in range(micros):
            pieces[m] = pieces[m] + [partner(part, step) for part in pieces[m]]
    late, pieces = lax.optimization_barrier((in_weight[:, inner * peers:], pieces))
    wg = lax.all_gather(mine(late), "dp", axis=0, tiled=True)
    wo = lax.all_gather(out_weight, "dp", axis=0, tiled=True)
    small = first[:, peers * rows:].reshape(groups, packed, share)
    at = states + KCONV + 3
    gain = small[:, at:at + gain_rows].reshape(1, width).astype(F32)
    small = jnp.concatenate([small[d] for d in range(groups)], axis=1)
    alog = small[0:states]
    at = states
    cw = small[at:at + KCONV].astype(F32)
    cb = small[at + KCONV:at + KCONV + 1].astype(F32)
    dtb = small[at + KCONV + 1:at + KCONV + 2].astype(F32)
    skip = small[at + KCONV + 2:at + KCONV + 3].astype(F32)
    dtw = small[2 * states:2 * states + rank]
    xw = small[2 * states + rank:]

    convs, normed = [], None
    for m in range(micros):
        normed, branch, x, proj = conv_forward(order, pieces[m], gain, first, cw, cb, xw, rank, m, micros, normed)
        proj = (proj + partner(proj, 1)).astype(BF16)
        if m + 1 < micros:
            proj, pieces[m + 1] = lax.optimization_barrier((proj, pieces[m + 1]))
        convs.append((branch, x, sum_over_pieces(proj)))
    positions = me * piece + jnp.arange(piece, dtype=jnp.int32)
    valid = (positions[None, :] < lengths).astype(F32)[..., None]
    own_grad = (valid * cotangent.astype(F32)).astype(BF16)
    y, starts = None, []
    for m in range(micros):
        y, start = scan_forward(order, convs[m][2], convs[m][1], dtw, dtb, alog, skip, m, micros, y)
        starts.append(start)
        if m == 0:
            grads, y, convs = lax.optimization_barrier(([own_grad], y, convs))
            for step in list(halvings())[:-1]:
                grads = grads + [partner(part, step) for part in grads]
    gate = dot(normed, wg, ((1,), (0,)))
    grads, y = lax.optimization_barrier((grads, y))
    grads = grads + [partner(part, 1) for part in grads]
    out_grad = jnp.concatenate(grads, axis=1).reshape(micros * length, width)
    gg = dot(out_grad, wo, ((1,), (1,)))
    sig = jax.nn.sigmoid(gate)
    yf = y.astype(F32)
    gated = (yf * gate * sig).astype(BF16)
    sg = (gg * gate * sig).astype(BF16)
    gate_grad = (gg * yf * sig * (1.0 + gate * (1.0 - sig))).astype(BF16)
    partial = dot(gated, wo, ((1,), (0,)), BF16).reshape(micros, length, width)
    gwo = dot(gated, out_grad, ((0,), (0,)), BF16)
    gwg = dot(normed, gate_grad, ((0,), (0,)), BF16)
    gwo, gwg, sg, partial = lax.optimization_barrier((gwo, gwg, sg, partial))
    gwo = lax.psum_scatter(gwo, "dp", scatter_dimension=0, tiled=True)
    gwg = lax.psum_scatter(gwg, "dp", scatter_dimension=0, tiled=True)
    gwg = lax.all_to_all(gwg, "seq", split_axis=0, concat_axis=0, tiled=True)
    added = sum_to_piece(partial, 1)
    backs = []
    for m in range(micros):
        given = sg
        if m == micros - 1:
            given, gwo, added = lax.optimization_barrier((given, gwo, added))
            result = (valid * (tokens.astype(F32) + added)).astype(BF16)
        backs.append(list(scan_backward(order, convs[m][2], convs[m][1], given, starts[m], dtw, dtb, alog, skip, m)))
        pg = (backs[m][0] + partner(backs[m][0], 1)).astype(BF16)
        backs[m][0] = sum_over_pieces(pg)
    for m in range(micros - 1):
        backs[m][0], backs[-1][1] = lax.optimization_barrier((backs[m][0], backs[-1][1]))
    w = dot(gate_grad, wg, ((1,), (1,)))
    w, backs[0][0] = lax.optimization_barrier((w, backs[0][0]))
    mixed, totals = None, None
    for m in range(micros):
        pg, xg, gdtw, gdtb, galog, gskip = backs[m]
        if m == micros - 1:
            pg, gwg = lax.optimization_barrier((pg, gwg))
        mixed, gxw, gcb, gcw = conv_backward(order, pg, xg, convs[m][0], convs[m][1], cw, cb, xw, m, micros, mixed)
        part = [galog, gcw, gcb, gdtb, gskip, gdtw, gxw]
        totals = part if totals is None else [a + b for a, b in zip(totals, part)]
    gwb = dot(normed, mixed, ((0,), (0,)), BF16)
    gwb, totals, mixed = lax.optimization_barrier((gwb, totals, mixed))
    gwb = lax.psum_scatter(gwb, "dp", scatter_dimension=0, tiled=True)
    gsmall = sum_to_owner(jnp.concatenate(totals, axis=0))
    wb = first[:, :peers * rows].reshape(width, inner)
    w = w + dot(mixed, wb, ((1,), (1,)))
    w = sum_to_piece(w.astype(BF16).reshape(micros, length, width), 1)
    w, gwb, gsmall = lax.optimization_barrier((w, gwb, gsmall))
    w = w * gain
    inputs = tokens.astype(F32)
    scale = lax.rsqrt(jnp.mean(inputs * inputs, axis=-1, keepdims=True) + EPSILON)
    input_grad = (own_grad.astype(F32) + scale * w - inputs * (scale * scale * scale)
                  * jnp.mean(w * inputs, axis=-1, keepdims=True)).astype(BF16)
    gwb = lax.all_to_all(gwb, "seq", split_axis=0, concat_axis=0, tiled=True)
    spread = lambda g: g.astype(F32).reshape(peers, rows, groups, share).transpose(1, 2, 0, 3).reshape(rows, inner * peers)
    total = jnp.concatenate([spread(gwb), spread(gwg)], axis=1)
    g_gain = jnp.sum(in_weight.astype(F32) * total, axis=1) / norm_gain.astype(F32)
    pieces, at = [], 0
    for count in (states, KCONV, 1, 1, 1, rank, cols):
        pieces.append(gsmall[at:at + count])
        at += count
    galog, gcw, gcb, gdtb, gskip, gdtw, gxw = pieces
    return (
        result[:, None], input_grad[:, None], g_gain, total, gcw, gcb[0], gxw.T, gdtw, gdtb[0], galog, gskip[0],
        gwo.astype(F32),
    )


def solution(mesh):
    placed = (
        P(None, "dp", "seq", None),
        P(None, "dp"),
        P(None, "dp", "seq", None),
        P(("dp", "seq")),
        P(("dp", "seq"), None),
        P(None, ("dp", "seq")),
        P(("dp", "seq")),
        P(("dp", "seq"), None),
        P(None, ("dp", "seq")),
        P(("dp", "seq")),
        P(None, ("dp", "seq")),
        P(("dp", "seq")),
        P(("dp", "seq"), None),
    )
    return jax.shard_map(
        body,
        mesh=mesh,
        in_specs=placed,
        out_specs=(
            P(None, "dp", "seq", None),
            P(None, "dp", "seq", None),
            P(("dp", "seq")),
            P(("dp", "seq"), None),
            P(None, ("dp", "seq")),
            P(("dp", "seq")),
            P(("dp", "seq"), None),
            P(None, ("dp", "seq")),
            P(("dp", "seq")),
            P(None, ("dp", "seq")),
            P(("dp", "seq")),
            P(("dp", "seq"), None),
        ),
        check_vma=False,
    )
```

```python
import jax
import jax.numpy as jnp
from jax import lax
from jax.experimental import pallas as pl
from jax.experimental.pallas import tpu as pltpu
from jax.sharding import PartitionSpec as P

F32 = jnp.float32
BF16 = jnp.bfloat16
LOG2E = 1.4426950408889634
CHUNK = 128
KCONV = 4
EPSILON = 1e-05
UNROLL = 16


def softplus(v):
    e = jnp.exp(-jnp.abs(v))
    series = e * (1.0 + e * (-0.5 + e * (1.0 / 3.0 - 0.25 * e)))
    return jnp.maximum(v, 0.0) + jnp.where(e < 0.0078125, series, jnp.log(1.0 + e))


def tree(values):
    while len(values) > 1:
        values = [a + b for a, b in zip(values[0::2], values[1::2])]
    return values[0]


def widen(value, width):
    return jnp.concatenate([value] * (width // 128), axis=1) if width > 128 else value


def own_token(tokens, states):
    row = lax.broadcasted_iota(jnp.int32, (tokens, UNROLL * states), 0) % UNROLL
    return row == lax.broadcasted_iota(jnp.int32, (tokens, UNROLL * states), 1) // states


def diagonal(maps):
    states, tokens = maps.shape
    column = lax.broadcasted_iota(jnp.int32, (states, UNROLL * states), 1) % states
    repeat = (column == lax.broadcasted_iota(jnp.int32, (states, UNROLL * states), 0)).astype(BF16)
    every = lax.dot_general(maps.astype(BF16), repeat, (((0,), (0,)), ((), ())), preferred_element_type=F32)
    return jnp.where(own_token(tokens, states), every, 0.0).astype(BF16)


def stagger(maps, out):
    states, tokens = maps.shape
    for i in range(tokens // UNROLL):
        at = (i + 1) * states
        out[at:at + states, :] = maps if i == 0 else pltpu.roll(maps, tokens - i * UNROLL, 1)


def lane_block(maps, group, states):
    return maps[pl.ds(pl.multiple_of((group + 1) * states, states), states), :]


def column(block, r):
    return jnp.broadcast_to(block[:, r:r + 1], (block.shape[0], 128))


def scan_forward_kernel(order, lengths, proj_ref, x_ref, dtw_ref, dtb_ref, alog_ref, skip_ref, held_ref,
                        y_ref, start_ref, state, steps, drive, ins, outs, spread, seen, ysum, *, width, micro):
    length, inner = x_ref.shape
    states = state.shape[0]
    live = pl.program_id(0) * length < lengths[micro]

    @pl.when(pl.program_id(0) == 0)
    def _():
        state[...] = jnp.zeros_like(state)

    @pl.when(jnp.logical_not(live))
    def _():
        y_ref[...] = jnp.zeros_like(y_ref)
        start_ref[...] = jnp.zeros_like(start_ref)

    @pl.when(live)
    def _():
        start_ref[0] = state[...]
        xs = x_ref[...].astype(F32)
        pre = jnp.dot(proj_ref[0:length, :].astype(BF16), dtw_ref[...], preferred_element_type=F32) + dtb_ref[...]
        step = softplus(pre)
        steps[...] = step
        drive[...] = step * xs
        stagger(proj_ref[length:length + states, :], ins)
        outs[UNROLL:UNROLL + length, :] = diagonal(proj_ref[length + states:length + 2 * states, :])
        for g in range(inner // width):
            lanes = slice(g * width, (g + 1) * width)
            rate = -jnp.exp(alog_ref[:, lanes].astype(F32)) * LOG2E
            for r in range(UNROLL):
                spread[r * states:(r + 1) * states, :] = column(ins[states:2 * states, :], r)

            def settle(group, slot):
                rows = pl.ds(pl.multiple_of(group * UNROLL, UNROLL), UNROLL)
                ysum[rows, lanes] = jnp.dot(outs[rows, :], seen[slot], preferred_element_type=F32)

            def advance(group, h, slot):
                base = pl.multiple_of(group * UNROLL, UNROLL)
                block = lane_block(ins, group + 1, states)
                for r in range(UNROLL):
                    st = steps[pl.ds(base + r, 1), lanes]
                    dr = drive[pl.ds(base + r, 1), lanes]
                    row = slice(r * states, (r + 1) * states)
                    h = jnp.exp2(st * rate) * h + widen(spread[row, :], width) * dr
                    spread[row, :] = column(block, r)
                    seen[slot, row, :] = h.astype(BF16)
                return h

            def pair(i, h):
                settle(2 * i, 1)
                h = advance(2 * i, h, 0)
                settle(2 * i + 1, 0)
                return advance(2 * i + 1, h, 1)

            state[:, lanes] = lax.fori_loop(0, length // UNROLL // 2, pair, state[:, lanes])
            settle(length // UNROLL, 1)
        y_ref[...] = (ysum[UNROLL:UNROLL + length, :] + skip_ref[...] * xs).astype(y_ref.dtype)


def spec_nat(length, cols):
    return pl.BlockSpec((length, cols), lambda i, order, lengths: (i, 0))


def whole_spec(shape):
    return pl.BlockSpec(shape, lambda i, order, lengths: (0,) * len(shape))


def placed(per_piece, count, micro, micros, reverse=False):
    def index(i, order, lengths):
        at = count - 1 - i if reverse else i
        return ((order[at // per_piece] * micros + micro) * per_piece + at % per_piece, 0)
    return index


def scan_forward(order, lengths, proj, x, dtw, dtb, alog, skip, micro, micros, held, width=512):
    length, inner = x.shape
    count = length // CHUNK
    states = alog.shape[0]
    rank = dtw.shape[0]
    per_piece = count // order.shape[0]
    width = min(width, inner)
    first = held is None
    return pl.pallas_call(
        lambda *refs: scan_forward_kernel(*refs, width=width, micro=micro),
        grid_spec=pltpu.PrefetchScalarGridSpec(
            num_scalar_prefetch=2,
            grid=(count,),
            in_specs=[
                spec_nat(CHUNK + 2 * states, rank), spec_nat(CHUNK, inner),
                whole_spec((rank, inner)), whole_spec((1, inner)), whole_spec((states, inner)), whole_spec((1, inner)),
                pl.BlockSpec(memory_space=pl.ANY),
            ],
            out_specs=[
                pl.BlockSpec((CHUNK, inner), placed(per_piece, count, micro, micros)),
                pl.BlockSpec((1, states, inner), lambda i, order, lengths: (i, 0, 0)),
            ],
            scratch_shapes=[
                pltpu.VMEM((states, inner), F32),
                pltpu.VMEM((CHUNK, inner), F32),
                pltpu.VMEM((CHUNK, inner), F32),
                pltpu.VMEM(((CHUNK // UNROLL + 2) * states, 128), F32),
                pltpu.VMEM((CHUNK + UNROLL, UNROLL * states), BF16),
                pltpu.VMEM((UNROLL * states, 128), F32),
                pltpu.VMEM((2, UNROLL * states, width), BF16),
                pltpu.VMEM((CHUNK + UNROLL, inner), F32),
            ],
        ),
        out_shape=[
            jax.ShapeDtypeStruct((micros * length, inner), BF16),
            jax.ShapeDtypeStruct((count, states, inner), F32),
        ],
        input_output_aliases={} if first else {8: 0},
        name="scan_forward",
    )(order, lengths, proj, x, dtw, dtb, alog, skip, dtb if first else held)


def scan_backward_kernel(order, lengths, proj_ref, x_ref, sg_ref, start_ref, dtw_ref, dtb_ref, alog_ref, skip_ref,
                         pg_ref, xg_ref, gdtw_ref, gdtb_ref, galog_ref, gskip_ref,
                         adjoint, steps, drive, grads, ins, outs, inmap, spread, seen, turns, hist, fac, bsum, csum,
                         lamb, stepg, *,
                         width, micro):
    length, inner = x_ref.shape
    states = adjoint.shape[0]
    at = pl.num_programs(0) - 1 - pl.program_id(0)
    live = at * length < lengths[micro]

    @pl.when(pl.program_id(0) == 0)
    def _():
        adjoint[...] = jnp.zeros_like(adjoint)
        gdtw_ref[...] = jnp.zeros_like(gdtw_ref)
        gdtb_ref[...] = jnp.zeros_like(gdtb_ref)
        galog_ref[...] = jnp.zeros_like(galog_ref)
        gskip_ref[...] = jnp.zeros_like(gskip_ref)

    @pl.when(jnp.logical_not(live))
    def _():
        pg_ref[...] = jnp.zeros_like(pg_ref)
        xg_ref[...] = jnp.zeros_like(xg_ref)

    @pl.when(live)
    def _():
        low = proj_ref[0:length, :].astype(BF16)
        pre = jnp.dot(low, dtw_ref[...], preferred_element_type=F32) + dtb_ref[...]
        step = softplus(pre)
        steps[...] = step
        drive[0:length, :] = step * x_ref[...].astype(F32)
        grads[...] = sg_ref[...].astype(F32)
        stagger(proj_ref[length:length + states, :], ins)
        stagger(proj_ref[length + states:length + 2 * states, :], outs)
        inmap[0:length, :] = diagonal(proj_ref[length:length + states, :])
        count = length // UNROLL
        for g in range(inner // width):
            lanes = slice(g * width, (g + 1) * width)
            decay = -jnp.exp(alog_ref[:, lanes].astype(F32))
            rate = decay * LOG2E
            for r in range(UNROLL):
                spread[r * states:(r + 1) * states, :] = column(ins[states:2 * states, :], r)

            def settle_states(group, slot):
                given = pl.ds(pl.multiple_of(jnp.maximum(group - 1, 0) * UNROLL, UNROLL), UNROLL)
                rows = pl.ds(pl.multiple_of(group * UNROLL, UNROLL), UNROLL)
                total = lax.dot_general(sg_ref[given, lanes], seen[slot], (((1,), (1,)), ((), ())),
                                        preferred_element_type=F32)
                csum[rows, :] = total if g == 0 else csum[rows, :] + total

            def advance(group, h, slot):
                base = pl.multiple_of(group * UNROLL, UNROLL)
                block = lane_block(ins, group + 1, states)
                for r in range(UNROLL):
                    st = steps[pl.ds(base + r, 1), lanes]
                    dr = drive[pl.ds(base + r, 1), lanes]
                    at = pl.ds(pl.multiple_of((base + r) * states, states), states)
                    row = slice(r * states, (r + 1) * states)
                    hist[at, :] = h
                    a = jnp.exp2(st * rate)
                    fac[at, :] = a
                    h = a * h + widen(spread[row, :], width) * dr
                    spread[row, :] = column(block, r)
                    seen[slot, row, :] = h.astype(BF16)
                return h

            def pair(i, h):
                settle_states(2 * i, 1)
                h = advance(2 * i, h, 0)
                settle_states(2 * i + 1, 0)
                return advance(2 * i + 1, h, 1)

            lax.fori_loop(0, count // 2, pair, start_ref[0, :, lanes])
            settle_states(count, 1)
            for r in range(UNROLL):
                spread[r * states:(r + 1) * states, :] = column(outs[count * states:(count + 1) * states, :], r)

            def settle_adjoints(group, slot):
                rows = pl.ds(pl.multiple_of(group * UNROLL, UNROLL), UNROLL)
                lamb[rows, lanes] = jnp.dot(inmap[rows, :], seen[slot], preferred_element_type=F32)
                total = lax.dot_general(drive[rows, lanes].astype(BF16), seen[slot], (((1,), (1,)), ((), ())),
                                        preferred_element_type=F32)
                bsum[rows, :] = total if g == 0 else bsum[rows, :] + total

            def retreat(group, adj, dsum, slot):
                base = pl.multiple_of(group * UNROLL, UNROLL)
                block = lane_block(outs, group - 1, states)
                for r in reversed(range(UNROLL)):
                    st = steps[pl.ds(base + r, 1), lanes]
                    sg = grads[pl.ds(base + r, 1), lanes]
                    at = pl.ds(pl.multiple_of((base + r) * states, states), states)
                    row = slice(r * states, (r + 1) * states)
                    lam = adj + widen(spread[row, :], width) * sg
                    spread[row, :] = column(block, r)
                    seen[slot, row, :] = lam.astype(BF16)
                    adj = fac[at, :] * lam
                    w = adj * hist[at, :]
                    dsum = dsum + w * st
                    q = w * decay
                    q = q[0:8] + q[8:16]
                    for k in range(width // 128):
                        turns[slot, k, r * 8:(r + 1) * 8, :] = q[:, k * 128:(k + 1) * 128]
                for k in range(width // 128):
                    for q in range(0, UNROLL, 8):
                        stepg[pl.ds(base + q, 8), g * width + k * 128:g * width + (k + 1) * 128] = tree(
                            [turns[slot, k, pl.ds(q * 8 + n, 8, stride=8), :] for n in range(8)])
                return adj, dsum

            def back_pair(i, carry):
                top = count - 1 - 2 * i
                settle_adjoints(top + 1, 1)
                carry = retreat(top, *carry, 0)
                settle_adjoints(top, 0)
                return retreat(top - 1, *carry, 1)

            adj, dsum = lax.fori_loop(0, count // 2, back_pair, (adjoint[:, lanes], jnp.zeros((states, width), F32)))
            settle_adjoints(0, 1)
            adjoint[:, lanes] = adj
            galog_ref[:, lanes] += dsum * decay
        xs = x_ref[...].astype(F32)
        sg = grads[...]
        lam_b = lamb[0:length, :]
        low = proj_ref[0:length, :].astype(BF16)
        pre = jnp.dot(low, dtw_ref[...], preferred_element_type=F32) + dtb_ref[...]
        pre_grad = (stepg[0:length, :] + xs * lam_b) * jax.nn.sigmoid(pre)
        gdtb_ref[...] += jnp.sum(pre_grad, axis=0, keepdims=True)
        gskip_ref[...] += jnp.sum(sg * xs, axis=0, keepdims=True)
        xg_ref[...] = (steps[...] * lam_b + skip_ref[...] * sg).astype(xg_ref.dtype)
        pre_low = pre_grad.astype(BF16)
        gdtw_ref[...] += lax.dot_general(low, pre_low, (((0,), (0,)), ((), ())), preferred_element_type=F32)
        pg_ref[0:length, :] = lax.dot_general(pre_low, dtw_ref[...], (((1,), (1,)), ((), ())), preferred_element_type=F32)
        mine = own_token(length, states)
        state = lax.broadcasted_iota(jnp.int32, (states, UNROLL * states), 1) % states
        pick = (state == lax.broadcasted_iota(jnp.int32, (states, UNROLL * states), 0)).astype(BF16)
        for row, sums in ((length, bsum[0:length, :]), (length + states, csum[UNROLL:UNROLL + length, :])):
            pg_ref[row:row + states, :] = lax.dot_general(
                pick, jnp.where(mine, sums, 0.0).astype(BF16), (((1,), (1,)), ((), ())), preferred_element_type=F32)


def scan_backward(order, lengths, proj, x, sg, starts, dtw, dtb, alog, skip, micro, micros, width=512):
    length, inner = x.shape
    count = length // CHUNK
    states = alog.shape[0]
    rank = dtw.shape[0]
    per_piece = count // order.shape[0]
    width = min(width, inner)
    rev = lambda cols: pl.BlockSpec((CHUNK, cols), lambda i, order, lengths: (count - 1 - i, 0))
    return pl.pallas_call(
        lambda *refs: scan_backward_kernel(*refs, width=width, micro=micro),
        grid_spec=pltpu.PrefetchScalarGridSpec(
            num_scalar_prefetch=2,
            grid=(count,),
            in_specs=[
                pl.BlockSpec((CHUNK + 2 * states, rank), lambda i, order, lengths: (count - 1 - i, 0)), rev(inner),
                pl.BlockSpec((CHUNK, inner), placed(per_piece, count, micro, micros, True)),
                pl.BlockSpec((1, states, inner), lambda i, order, lengths: (count - 1 - i, 0, 0)),
                whole_spec((rank, inner)), whole_spec((1, inner)), whole_spec((states, inner)), whole_spec((1, inner)),
            ],
            out_specs=[
                pl.BlockSpec((CHUNK + 2 * states, rank), lambda i, order, lengths: (count - 1 - i, 0)),
                rev(inner),
                whole_spec((rank, inner)), whole_spec((1, inner)), whole_spec((states, inner)), whole_spec((1, inner)),
            ],
            scratch_shapes=[
                pltpu.VMEM((states, inner), F32),
                pltpu.VMEM((CHUNK, inner), F32),
                pltpu.VMEM((CHUNK + UNROLL, inner), F32),
                pltpu.VMEM((CHUNK, inner), F32),
                pltpu.VMEM(((CHUNK // UNROLL + 2) * states, 128), F32),
                pltpu.VMEM(((CHUNK // UNROLL + 2) * states, 128), F32),
                pltpu.VMEM((CHUNK + UNROLL, UNROLL * states), BF16),
                pltpu.VMEM((UNROLL * states, 128), F32),
                pltpu.VMEM((2, UNROLL * states, width), BF16),
                pltpu.VMEM((2, width // 128, 8 * UNROLL, 128), F32),
                pltpu.VMEM((CHUNK * states, width), F32),
                pltpu.VMEM((CHUNK * states, width), F32),
                pltpu.VMEM((CHUNK + UNROLL, UNROLL * states), F32),
                pltpu.VMEM((CHUNK + UNROLL, UNROLL * states), F32),
                pltpu.VMEM((CHUNK + UNROLL, inner), F32),
                pltpu.VMEM((CHUNK + UNROLL, inner), F32),
            ],
        ),
        out_shape=[
            jax.ShapeDtypeStruct((count * (CHUNK + 2 * states), rank), F32),
            jax.ShapeDtypeStruct((length, inner), BF16),
            jax.ShapeDtypeStruct((rank, inner), F32),
            jax.ShapeDtypeStruct((1, inner), F32),
            jax.ShapeDtypeStruct((states, inner), F32),
            jax.ShapeDtypeStruct((1, inner), F32),
        ],
        name="scan_backward",
    )(order, lengths, proj, x, sg, starts, dtw, dtb, alog, skip)


def conv_forward_kernel(order, lengths, *refs, peers, micro):
    pieces = refs[:peers]
    gain_ref, wb_ref, cw_ref, cb_ref, xw_ref, held_ref, normed_ref, branch_ref, x_ref, proj_ref, pad = refs[peers:]
    length, inner = x_ref.shape
    at = pl.program_id(0)

    @pl.when(at == 0)
    def _():
        pad[0:8, :] = jnp.zeros((8, inner), F32)

    live = at * length < lengths[micro]

    @pl.when(jnp.logical_not(live))
    def _():
        for ref in (normed_ref, branch_ref, x_ref, proj_ref):
            ref[...] = jnp.zeros_like(ref)

    for p in range(peers):
        @pl.when(jnp.logical_and(live, order[at] == p))
        def _():
            tokens = pieces[p][...].astype(F32)
            scale = lax.rsqrt(jnp.mean(tokens * tokens, axis=-1, keepdims=True) + EPSILON)
            normed_ref[...] = (tokens * scale * gain_ref[...]).astype(BF16)

    @pl.when(live)
    def _():
        groups = wb_ref.shape[0]
        deep = normed_ref.shape[1] // groups
        branch = sum(jnp.dot(normed_ref[:, d * deep:(d + 1) * deep], wb_ref[d, 0:deep, :], preferred_element_type=F32)
                     for d in range(groups)).astype(BF16)
        branch_ref[...] = branch
        pad[8:8 + length, :] = branch.astype(F32)
        pre = cb_ref[...] + sum(cw_ref[k:k + 1, :] * pad[5 + k:5 + k + length, :] for k in range(KCONV))
        x = (pre * jax.nn.sigmoid(pre)).astype(BF16)
        x_ref[...] = x
        rank = proj_ref.shape[1]
        low = lax.dot_general(x, xw_ref[0:rank, :], (((1,), (1,)), ((), ())), preferred_element_type=F32)
        maps = lax.dot_general(xw_ref[rank:, :], x, (((1,), (1,)), ((), ())), preferred_element_type=F32)
        rows = CHUNK + maps.shape[0]
        for k in range(length // CHUNK):
            proj_ref[k * rows:k * rows + CHUNK, :] = low[k * CHUNK:(k + 1) * CHUNK, :]
            proj_ref[k * rows + CHUNK:(k + 1) * rows, :] = maps[:, k * CHUNK:(k + 1) * CHUNK]
        pad[0:8, :] = pad[length:length + 8, :]


def conv_forward(order, lengths, pieces, gain, wb, cw, cb, xw, rank, micro, micros, held):
    peers = len(pieces)
    tokens, width = pieces[0].shape
    inner = wb.shape[2]
    cols = xw.shape[0]
    rows = tokens // CHUNK * (CHUNK + cols - rank)
    first = held is None
    return pl.pallas_call(
        lambda *refs: conv_forward_kernel(*refs, peers=peers, micro=micro),
        grid_spec=pltpu.PrefetchScalarGridSpec(
            num_scalar_prefetch=2,
            grid=(peers,),
            in_specs=[whole_spec((tokens, width))] * peers + [
                whole_spec((1, width)),
                whole_spec(wb.shape), whole_spec((KCONV, inner)), whole_spec((1, inner)), whole_spec((cols, inner)),
                pl.BlockSpec(memory_space=pl.ANY),
            ],
            out_specs=[
                pl.BlockSpec((tokens, width), placed(1, peers, micro, micros)),
                spec_nat(tokens, inner), spec_nat(tokens, inner), spec_nat(rows, rank),
            ],
            scratch_shapes=[pltpu.VMEM((tokens + 8, inner), F32)],
        ),
        out_shape=[
            jax.ShapeDtypeStruct((micros * peers * tokens, width), BF16),
            jax.ShapeDtypeStruct((peers * tokens, inner), BF16),
            jax.ShapeDtypeStruct((peers * tokens, inner), BF16),
            jax.ShapeDtypeStruct((peers * rows, rank), F32),
        ],
        input_output_aliases={} if first else {peers + 7: 0},
        name="conv_forward",
    )(order, lengths, *pieces, gain, wb, cw, cb, xw, gain if first else held)


def conv_backward_kernel(order, lengths, pg_ref, xg_ref, branch_ref, prev_ref, x_ref, cw_ref, cb_ref, xw_ref, held_ref,
                         mixed_ref, gxw_ref, gcb_ref, gcw_ref, pad, ahead, *, micro):
    length, inner = x_ref.shape

    @pl.when(pl.program_id(0) == 0)
    def _():
        ahead[length:length + 8, :] = jnp.zeros((8, inner), F32)
        gxw_ref[...] = jnp.zeros_like(gxw_ref)
        gcb_ref[...] = jnp.zeros_like(gcb_ref)
        gcw_ref[...] = jnp.zeros_like(gcw_ref)

    at = pl.num_programs(0) - 1 - pl.program_id(0)
    live = at * length < lengths[micro]

    @pl.when(jnp.logical_not(live))
    def _():
        mixed_ref[...] = jnp.zeros_like(mixed_ref)

    @pl.when(live)
    def _():
        earliest = pl.program_id(0) == pl.num_programs(0) - 1
        pad[0:8, :] = jnp.where(earliest, 0.0, prev_ref[...].astype(F32)[8:16, :])
        pad[8:8 + length, :] = branch_ref[...].astype(F32)
        pre = cb_ref[...] + sum(cw_ref[k:k + 1, :] * pad[5 + k:5 + k + length, :] for k in range(KCONV))
        sig = jax.nn.sigmoid(pre)
        rank = pg_ref.shape[1]
        rows = CHUNK + xw_ref.shape[0] - rank
        low, maps = [], []
        for k in range(length // CHUNK):
            low.append(pg_ref[k * rows:k * rows + CHUNK, :].astype(BF16))
            maps.append(pg_ref[k * rows + CHUNK:(k + 1) * rows, :].astype(BF16))
        low, maps = jnp.concatenate(low, axis=0), jnp.concatenate(maps, axis=1)
        grad = (jnp.dot(low, xw_ref[0:rank, :], preferred_element_type=F32)
                + lax.dot_general(maps, xw_ref[rank:, :], (((0,), (0,)), ((), ())), preferred_element_type=F32)
                + xg_ref[...].astype(F32))
        grad = grad * (sig * (1.0 + pre * (1.0 - sig)))
        ahead[0:length, :] = grad
        gcb_ref[...] += jnp.sum(grad, axis=0, keepdims=True)
        for k in range(KCONV):
            gcw_ref[k:k + 1, :] += jnp.sum(grad * pad[5 + k:5 + k + length, :], axis=0, keepdims=True)
        mixed = sum(cw_ref[k:k + 1, :] * ahead[3 - k:3 - k + length, :] for k in range(KCONV))
        mixed_ref[...] = mixed.astype(BF16)
        gxw_ref[0:rank, :] += lax.dot_general(low, x_ref[...], (((0,), (0,)), ((), ())), preferred_element_type=F32)
        gxw_ref[rank:, :] += jnp.dot(maps, x_ref[...], preferred_element_type=F32)
        ahead[length:length + 8, :] = ahead[0:8, :]


def conv_backward(order, lengths, pg, xg, branch, x, cw, cb, xw, micro, micros, held):
    length, inner = x.shape
    tokens = length // order.shape[0]
    count = length // tokens
    cols = xw.shape[0]
    first = held is None
    rank = pg.shape[1]
    rows = pg.shape[0] // count
    rev = lambda width: pl.BlockSpec((tokens, width), lambda i, order, lengths: (count - 1 - i, 0))
    return pl.pallas_call(
        lambda *refs: conv_backward_kernel(*refs, micro=micro),
        grid_spec=pltpu.PrefetchScalarGridSpec(
            num_scalar_prefetch=2,
            grid=(count,),
            in_specs=[
                pl.BlockSpec((rows, rank), lambda i, order, lengths: (count - 1 - i, 0)), rev(inner), rev(inner),
                pl.BlockSpec((16, inner), lambda i, order, lengths: (jnp.maximum((count - 1 - i) * (tokens // 16) - 1, 0), 0)),
                rev(inner),
                whole_spec((KCONV, inner)), whole_spec((1, inner)), whole_spec((cols, inner)),
                pl.BlockSpec(memory_space=pl.ANY),
            ],
            out_specs=[
                pl.BlockSpec((tokens, inner), placed(1, count, micro, micros, True)),
                whole_spec((cols, inner)), whole_spec((1, inner)), whole_spec((KCONV, inner)),
            ],
            scratch_shapes=[pltpu.VMEM((tokens + 8, inner), F32), pltpu.VMEM((tokens + 8, inner), F32)],
        ),
        out_shape=[
            jax.ShapeDtypeStruct((micros * length, inner), BF16),
            jax.ShapeDtypeStruct((cols, inner), F32),
            jax.ShapeDtypeStruct((1, inner), F32),
            jax.ShapeDtypeStruct((KCONV, inner), F32),
        ],
        input_output_aliases={} if first else {10: 0},
        name="conv_backward",
    )(order, lengths, pg, xg, branch, branch, x, cw, cb, xw, cb if first else held)


def partner(value, step):
    peers = lax.axis_size("seq")
    return lax.ppermute(value, "seq", [(i, i ^ step) for i in range(peers)])


def halvings():
    step = lax.axis_size("seq") // 2
    while step >= 1:
        yield step
        step //= 2


def reversed_bits(value, peers):
    out = value * 0
    step = 1
    while step < peers:
        out = out * 2 + (value // step) % 2
        step *= 2
    return out


def finish_piece(value):
    for step in reversed(list(halvings())[:-1]):
        half = value.shape[0] // 2
        value = value[:half].astype(F32) + partner(value[half:], step).astype(F32)
        value = value if step == lax.axis_size("seq") // 2 else value.astype(BF16)
    return value


def sum_over_pieces(value):
    for step in reversed(list(halvings())[:-1]):
        value = value.astype(F32) + partner(value, step).astype(F32)
        value = value if step == lax.axis_size("seq") // 2 else value.astype(BF16)
    return value


def sum_to_owner(whole):
    ranks = lax.axis_size("dp")
    me = lax.axis_index("dp")
    share = whole.shape[1] // ranks
    parts = jnp.stack([lax.dynamic_slice_in_dim(whole, (me ^ r) * share, share, 1) for r in range(ranks)]).astype(F32)
    step = 1
    while parts.shape[0] > 1:
        parts = parts.reshape((parts.shape[0] // 2, 2) + parts.shape[1:])
        given = parts[:, 1].astype(BF16)
        other = lax.ppermute(given, "dp", [(i, i ^ step) for i in range(ranks)])
        parts = parts[:, 0] + other.astype(F32)
        step *= 2
    return parts[0]


def dot(left, right, dims, kind=F32):
    return lax.dot_general(left, right, (dims, ((), ())), preferred_element_type=kind)


def body(tokens, lengths, cotangent, norm_gain, in_weight, conv_weight, conv_bias, x_weight, dt_weight,
         dt_bias, a_log, skip_d, out_weight):
    micros, slots, piece, width = tokens.shape
    peers, groups = lax.axis_size("seq"), lax.axis_size("dp")
    me = lax.axis_index("seq")
    share = conv_bias.shape[0]
    inner = share * groups
    rows = in_weight.shape[0]
    rank = dt_weight.shape[0]
    states = a_log.shape[0]
    cols = x_weight.shape[1]
    length = piece * peers
    order = reversed_bits(jnp.arange(peers, dtype=jnp.int32) ^ me, peers)
    tokens, cotangent = tokens[:, 0], cotangent[:, 0]
    held = lengths[:, 0]

    gain_part = norm_gain
    for step in halvings():
        gain_part = jnp.concatenate([gain_part, partner(gain_part, step)])
    gain_part = gain_part.reshape(peers, rows)
    gain_part = jnp.concatenate([lax.dynamic_slice_in_dim(gain_part, order[q], 1) for q in range(peers)])
    gain_rows = peers * rows // share
    small = jnp.concatenate([
        a_log, conv_weight, conv_bias[None], dt_bias[None], skip_d[None], gain_part.reshape(gain_rows, share),
        jnp.zeros((states - KCONV - 3 - gain_rows, share), BF16), dt_weight, x_weight.T], axis=0)
    packed = small.shape[0]

    def mine(half):
        own = half.reshape(rows, groups, peers, share).transpose(2, 0, 1, 3).reshape(peers * rows, inner)
        return lax.all_to_all(own, "seq", split_axis=0, concat_axis=0, tiled=True)

    first = jnp.concatenate([mine(in_weight[:, :inner * peers]), small.reshape(-1, inner)], axis=0)
    first = lax.all_gather(first, "dp", axis=0, tiled=False)
    pieces = [[tokens[m]] for m in range(micros)]
    for step in halvings():
        for m in range(micros):
            pieces[m] = pieces[m] + [partner(part, step) for part in pieces[m]]
    late, pieces = lax.optimization_barrier((in_weight[:, inner * peers:], pieces))
    wg = lax.all_gather(mine(late), "dp", axis=0, tiled=True)
    wo = lax.all_gather(out_weight, "dp", axis=0, tiled=True)
    small = first[:, peers * rows:].reshape(groups, packed, share)
    at = states + KCONV + 3
    gain = small[:, at:at + gain_rows].reshape(1, width).astype(F32)
    small = jnp.concatenate([small[d] for d in range(groups)], axis=1)
    alog = small[0:states]
    at = states
    cw = small[at:at + KCONV].astype(F32)
    cb = small[at + KCONV:at + KCONV + 1].astype(F32)
    dtb = small[at + KCONV + 1:at + KCONV + 2].astype(F32)
    skip = small[at + KCONV + 2:at + KCONV + 3].astype(F32)
    dtw = small[2 * states:2 * states + rank]
    xw = small[2 * states + rank:]

    cotangent, pieces = lax.optimization_barrier((cotangent, pieces))
    positions = me * piece + jnp.arange(piece, dtype=jnp.int32)
    valid = (positions[None, :] < lengths).astype(F32)[..., None]
    own_grad = (valid * cotangent.astype(F32)).astype(BF16)
    grads = [own_grad]
    for step in list(halvings())[:-1]:
        grads = grads + [partner(part, step) for part in grads]
    convs, normed = [], None
    for m in range(micros):
        normed, branch, x, proj = conv_forward(order, held, pieces[m], gain, first, cw, cb, xw, rank, m, micros, normed)
        proj = (proj + partner(proj, 1)).astype(BF16)
        if m + 1 < micros:
            proj, pieces[m + 1], grads = lax.optimization_barrier((proj, pieces[m + 1], grads))
        convs.append((branch, x, sum_over_pieces(proj)))
    grads = grads + [partner(part, 1) for part in grads]
    y, starts = None, []
    for m in range(micros):
        y, start = scan_forward(order, held, convs[m][2], convs[m][1], dtw, dtb, alog, skip, m, micros, y)
        starts.append(start)
    normed, y = lax.optimization_barrier((normed, y))
    gate = dot(normed, wg, ((1,), (0,)))
    sig = jax.nn.sigmoid(gate)
    yf = y.astype(F32)
    gated = (yf * gate * sig).astype(BF16)
    out_grad = jnp.concatenate(grads, axis=0).reshape(micros * length, width)
    gwo = dot(gated, out_grad, ((0,), (0,)), BF16)
    gwo, gated, out_grad = lax.optimization_barrier((gwo, gated, out_grad))
    gg = dot(out_grad, wo, ((1,), (1,)))
    sg = (gg * gate * sig).astype(BF16)
    gate_grad = (gg * yf * sig * (1.0 + gate * (1.0 - sig))).astype(BF16)
    half = micros * length // 2
    given = dot(gated[half:], wo, ((1,), (0,)), BF16)
    kept = dot(gated[:half], wo, ((1,), (0,)), BF16)
    given, kept, gate_grad = lax.optimization_barrier((given, kept, gate_grad))
    gwg = dot(normed, gate_grad, ((0,), (0,)), BF16)
    added = (kept.astype(F32) + partner(given, 1).astype(F32)).astype(BF16)
    gwg, sg, added = lax.optimization_barrier((gwg, sg, added))
    added = finish_piece(added)
    gwo = lax.psum_scatter(gwo, "dp", scatter_dimension=0, tiled=True)
    gwg = lax.psum_scatter(gwg, "dp", scatter_dimension=0, tiled=True)
    gwg = lax.all_to_all(gwg, "seq", split_axis=0, concat_axis=0, tiled=True)
    backs = []
    for m in range(micros):
        given = sg
        if m == micros - 1:
            given, gwo, added = lax.optimization_barrier((given, gwo, added))
            result = (valid * (tokens.astype(F32) + added.reshape(micros, piece, width))).astype(BF16)
        backs.append(list(scan_backward(
            order, held, convs[m][2], convs[m][1], given, starts[m], dtw, dtb, alog, skip, m, micros)))
        backs[m][0] = (backs[m][0] + partner(backs[m][0], 1)).astype(BF16)
        if m + 1 < micros:
            backs[m][0] = sum_over_pieces(backs[m][0])
    for m in range(micros - 1):
        backs[m][0], backs[-1][1] = lax.optimization_barrier((backs[m][0], backs[-1][1]))
    mixed, totals = None, None
    for m in range(micros):
        pg, xg, gdtw, gdtb, galog, gskip = backs[m]
        if m == micros - 1:
            pg, mixed, gate_grad = lax.optimization_barrier((pg, mixed, gate_grad))
            pg = sum_over_pieces(pg)
            early = dot(gate_grad, wg, ((1,), (1,)))
            pg, gwg, early = lax.optimization_barrier((pg, gwg, early))
        mixed, gxw, gcb, gcw = conv_backward(
            order, held, pg, xg, convs[m][0], convs[m][1], cw, cb, xw, m, micros, mixed)
        part = [galog, gcw, gcb, gdtb, gskip, gdtw, gxw]
        totals = part if totals is None else [a + b for a, b in zip(totals, part)]
    gwb = dot(normed, mixed, ((0,), (0,)), BF16)
    gwb, totals, mixed = lax.optimization_barrier((gwb, totals, mixed))
    gwb = lax.psum_scatter(gwb, "dp", scatter_dimension=0, tiled=True)
    gsmall = sum_to_owner(jnp.concatenate(totals, axis=0))
    wb = first[:, :peers * rows].reshape(width, inner)
    w = (early + dot(mixed, wb, ((1,), (1,)))).astype(BF16)
    w = finish_piece((w[:half].astype(F32) + partner(w[half:], 1).astype(F32)).astype(BF16)).reshape(micros, piece, width)
    w, gwb, gsmall = lax.optimization_barrier((w, gwb, gsmall))
    w = w * gain
    inputs = tokens.astype(F32)
    scale = lax.rsqrt(jnp.mean(inputs * inputs, axis=-1, keepdims=True) + EPSILON)
    input_grad = (own_grad.astype(F32) + scale * w - inputs * (scale * scale * scale)
                  * jnp.mean(w * inputs, axis=-1, keepdims=True)).astype(BF16)
    gwb = lax.all_to_all(gwb, "seq", split_axis=0, concat_axis=0, tiled=True)
    spread = lambda g: g.astype(F32).reshape(peers, rows, groups, share).transpose(1, 2, 0, 3).reshape(rows, inner * peers)
    total = jnp.concatenate([spread(gwb), spread(gwg)], axis=1)
    g_gain = jnp.sum(in_weight.astype(F32) * total, axis=1) / norm_gain.astype(F32)
    pieces, at = [], 0
    for count in (states, KCONV, 1, 1, 1, rank, cols):
        pieces.append(gsmall[at:at + count])
        at += count
    galog, gcw, gcb, gdtb, gskip, gdtw, gxw = pieces
    return (
        result[:, None], input_grad[:, None], g_gain, total, gcw, gcb[0], gxw.T, gdtw, gdtb[0], galog, gskip[0],
        gwo.astype(F32),
    )


def solution(mesh):
    placed = (
        P(None, "dp", "seq", None),
        P(None, "dp"),
        P(None, "dp", "seq", None),
        P(("dp", "seq")),
        P(("dp", "seq"), None),
        P(None, ("dp", "seq")),
        P(("dp", "seq")),
        P(("dp", "seq"), None),
        P(None, ("dp", "seq")),
        P(("dp", "seq")),
        P(None, ("dp", "seq")),
        P(("dp", "seq")),
        P(("dp", "seq"), None),
    )
    return jax.shard_map(
        body,
        mesh=mesh,
        in_specs=placed,
        out_specs=(
            P(None, "dp", "seq", None),
            P(None, "dp", "seq", None),
            P(("dp", "seq")),
            P(("dp", "seq"), None),
            P(None, ("dp", "seq")),
            P(("dp", "seq")),
            P(("dp", "seq"), None),
            P(None, ("dp", "seq")),
            P(("dp", "seq")),
            P(None, ("dp", "seq")),
            P(("dp", "seq")),
            P(("dp", "seq"), None),
        ),
        check_vma=False,
    )
```

```python
import jax
import jax.numpy as jnp
from jax import lax
from jax.experimental import pallas as pl
from jax.experimental.pallas import tpu as pltpu
from jax.sharding import PartitionSpec as P

F32 = jnp.float32
BF16 = jnp.bfloat16
LOG2E = 1.4426950408889634
CHUNK = 128
KCONV = 4
EPSILON = 1e-05
UNROLL = 16


def softplus(v):
    e = jnp.exp(-jnp.abs(v))
    series = e * (1.0 + e * (-0.5 + e * (1.0 / 3.0 - 0.25 * e)))
    return jnp.maximum(v, 0.0) + jnp.where(e < 0.0078125, series, jnp.log(1.0 + e))


def tree(values):
    while len(values) > 1:
        values = [a + b for a, b in zip(values[0::2], values[1::2])]
    return values[0]


def widen(value, width):
    return jnp.concatenate([value] * (width // 128), axis=1) if width > 128 else value


def own_token(tokens, states):
    row = lax.broadcasted_iota(jnp.int32, (tokens, UNROLL * states), 0) % UNROLL
    return row == lax.broadcasted_iota(jnp.int32, (tokens, UNROLL * states), 1) // states


def diagonal(maps):
    states, tokens = maps.shape
    column = lax.broadcasted_iota(jnp.int32, (states, UNROLL * states), 1) % states
    repeat = (column == lax.broadcasted_iota(jnp.int32, (states, UNROLL * states), 0)).astype(BF16)
    every = lax.dot_general(maps.astype(BF16), repeat, (((0,), (0,)), ((), ())), preferred_element_type=F32)
    return jnp.where(own_token(tokens, states), every, 0.0).astype(BF16)


def stagger(maps, out):
    states, tokens = maps.shape
    for i in range(tokens // UNROLL):
        at = (i + 1) * states
        out[at:at + states, :] = maps if i == 0 else pltpu.roll(maps, tokens - i * UNROLL, 1)


def lane_block(maps, group, states):
    return maps[pl.ds(pl.multiple_of((group + 1) * states, states), states), :]


def column(block, r):
    return jnp.broadcast_to(block[:, r:r + 1], (block.shape[0], 128))


def scan_forward_kernel(order, lengths, proj_ref, x_ref, dtw_ref, dtb_ref, alog_ref, skip_ref, held_ref,
                        y_ref, start_ref, state, steps, drive, ins, outs, spread, seen, ysum, *, width, micro):
    length, inner = x_ref.shape
    states = state.shape[0]
    live = pl.program_id(0) * length < lengths[micro]

    @pl.when(pl.program_id(0) == 0)
    def _():
        state[...] = jnp.zeros_like(state)

    @pl.when(jnp.logical_not(live))
    def _():
        y_ref[...] = jnp.zeros_like(y_ref)
        start_ref[...] = jnp.zeros_like(start_ref)

    @pl.when(live)
    def _():
        start_ref[0] = state[...]
        xs = x_ref[...].astype(F32)
        pre = jnp.dot(proj_ref[0:length, :].astype(BF16), dtw_ref[...], preferred_element_type=F32) + dtb_ref[...]
        step = softplus(pre)
        steps[...] = step
        drive[...] = step * xs
        stagger(proj_ref[length:length + states, :], ins)
        outs[UNROLL:UNROLL + length, :] = diagonal(proj_ref[length + states:length + 2 * states, :])
        for g in range(inner // width):
            lanes = slice(g * width, (g + 1) * width)
            rate = -jnp.exp(alog_ref[:, lanes].astype(F32)) * LOG2E
            for r in range(UNROLL):
                spread[r * states:(r + 1) * states, :] = column(ins[states:2 * states, :], r)

            def settle(group, slot):
                rows = pl.ds(pl.multiple_of(group * UNROLL, UNROLL), UNROLL)
                ysum[rows, lanes] = jnp.dot(outs[rows, :], seen[slot], preferred_element_type=F32)

            def advance(group, h, slot):
                base = pl.multiple_of(group * UNROLL, UNROLL)
                block = lane_block(ins, group + 1, states)
                for r in range(UNROLL):
                    st = steps[pl.ds(base + r, 1), lanes]
                    dr = drive[pl.ds(base + r, 1), lanes]
                    row = slice(r * states, (r + 1) * states)
                    h = jnp.exp2(st * rate) * h + widen(spread[row, :], width) * dr
                    spread[row, :] = column(block, r)
                    seen[slot, row, :] = h.astype(BF16)
                return h

            def pair(i, h):
                settle(2 * i, 1)
                h = advance(2 * i, h, 0)
                settle(2 * i + 1, 0)
                return advance(2 * i + 1, h, 1)

            state[:, lanes] = lax.fori_loop(0, length // UNROLL // 2, pair, state[:, lanes])
            settle(length // UNROLL, 1)
        y_ref[...] = (ysum[UNROLL:UNROLL + length, :] + skip_ref[...] * xs).astype(y_ref.dtype)


def spec_nat(length, cols):
    return pl.BlockSpec((length, cols), lambda i, order, lengths: (i, 0))


def whole_spec(shape):
    return pl.BlockSpec(shape, lambda i, order, lengths: (0,) * len(shape))


def placed(per_piece, count, micro, micros, reverse=False):
    def index(i, order, lengths):
        at = count - 1 - i if reverse else i
        return ((order[at // per_piece] * micros + micro) * per_piece + at % per_piece, 0)
    return index


def scan_forward(order, lengths, proj, x, dtw, dtb, alog, skip, micro, micros, held, width=512):
    length, inner = x.shape
    count = length // CHUNK
    states = alog.shape[0]
    rank = dtw.shape[0]
    per_piece = count // order.shape[0]
    width = min(width, inner)
    first = held is None
    return pl.pallas_call(
        lambda *refs: scan_forward_kernel(*refs, width=width, micro=micro),
        grid_spec=pltpu.PrefetchScalarGridSpec(
            num_scalar_prefetch=2,
            grid=(count,),
            in_specs=[
                spec_nat(CHUNK + 2 * states, rank), spec_nat(CHUNK, inner),
                whole_spec((rank, inner)), whole_spec((1, inner)), whole_spec((states, inner)), whole_spec((1, inner)),
                pl.BlockSpec(memory_space=pl.ANY),
            ],
            out_specs=[
                pl.BlockSpec((CHUNK, inner), placed(per_piece, count, micro, micros)),
                pl.BlockSpec((1, states, inner), lambda i, order, lengths: (i, 0, 0)),
            ],
            scratch_shapes=[
                pltpu.VMEM((states, inner), F32),
                pltpu.VMEM((CHUNK, inner), F32),
                pltpu.VMEM((CHUNK, inner), F32),
                pltpu.VMEM(((CHUNK // UNROLL + 2) * states, 128), F32),
                pltpu.VMEM((CHUNK + UNROLL, UNROLL * states), BF16),
                pltpu.VMEM((UNROLL * states, 128), F32),
                pltpu.VMEM((2, UNROLL * states, width), BF16),
                pltpu.VMEM((CHUNK + UNROLL, inner), F32),
            ],
        ),
        out_shape=[
            jax.ShapeDtypeStruct((micros * length, inner), BF16),
            jax.ShapeDtypeStruct((count, states, inner), F32),
        ],
        input_output_aliases={} if first else {8: 0},
        name="scan_forward",
    )(order, lengths, proj, x, dtw, dtb, alog, skip, dtb if first else held)


def scan_backward_kernel(order, lengths, proj_ref, x_ref, sg_ref, start_ref, dtw_ref, dtb_ref, alog_ref, skip_ref,
                         pg_ref, xg_ref, gdtw_ref, gdtb_ref, galog_ref, gskip_ref,
                         adjoint, steps, drive, grads, ins, outs, inmap, spread, seen, turns, hist, fac, bsum, csum,
                         lamb, stepg, *,
                         width, micro):
    length, inner = x_ref.shape
    states = adjoint.shape[0]
    at = pl.num_programs(0) - 1 - pl.program_id(0)
    live = at * length < lengths[micro]

    @pl.when(pl.program_id(0) == 0)
    def _():
        adjoint[...] = jnp.zeros_like(adjoint)
        gdtw_ref[...] = jnp.zeros_like(gdtw_ref)
        gdtb_ref[...] = jnp.zeros_like(gdtb_ref)
        galog_ref[...] = jnp.zeros_like(galog_ref)
        gskip_ref[...] = jnp.zeros_like(gskip_ref)

    @pl.when(jnp.logical_not(live))
    def _():
        pg_ref[...] = jnp.zeros_like(pg_ref)
        xg_ref[...] = jnp.zeros_like(xg_ref)

    @pl.when(live)
    def _():
        low = proj_ref[0:length, :].astype(BF16)
        pre = jnp.dot(low, dtw_ref[...], preferred_element_type=F32) + dtb_ref[...]
        step = softplus(pre)
        steps[...] = step
        drive[0:length, :] = step * x_ref[...].astype(F32)
        grads[...] = sg_ref[...].astype(F32)
        stagger(proj_ref[length:length + states, :], ins)
        stagger(proj_ref[length + states:length + 2 * states, :], outs)
        inmap[0:length, :] = diagonal(proj_ref[length:length + states, :])
        count = length // UNROLL
        for g in range(inner // width):
            lanes = slice(g * width, (g + 1) * width)
            decay = -jnp.exp(alog_ref[:, lanes].astype(F32))
            rate = decay * LOG2E
            for r in range(UNROLL):
                spread[r * states:(r + 1) * states, :] = column(ins[states:2 * states, :], r)

            def settle_states(group, slot):
                given = pl.ds(pl.multiple_of(jnp.maximum(group - 1, 0) * UNROLL, UNROLL), UNROLL)
                rows = pl.ds(pl.multiple_of(group * UNROLL, UNROLL), UNROLL)
                total = lax.dot_general(sg_ref[given, lanes], seen[slot], (((1,), (1,)), ((), ())),
                                        preferred_element_type=F32)
                csum[rows, :] = total if g == 0 else csum[rows, :] + total

            def advance(group, h, slot):
                base = pl.multiple_of(group * UNROLL, UNROLL)
                block = lane_block(ins, group + 1, states)
                for r in range(UNROLL):
                    st = steps[pl.ds(base + r, 1), lanes]
                    dr = drive[pl.ds(base + r, 1), lanes]
                    at = pl.ds(pl.multiple_of((base + r) * states, states), states)
                    row = slice(r * states, (r + 1) * states)
                    hist[at, :] = h
                    a = jnp.exp2(st * rate)
                    fac[at, :] = a
                    h = a * h + widen(spread[row, :], width) * dr
                    spread[row, :] = column(block, r)
                    seen[slot, row, :] = h.astype(BF16)
                return h

            def pair(i, h):
                settle_states(2 * i, 1)
                h = advance(2 * i, h, 0)
                settle_states(2 * i + 1, 0)
                return advance(2 * i + 1, h, 1)

            lax.fori_loop(0, count // 2, pair, start_ref[0, :, lanes])
            settle_states(count, 1)
            for r in range(UNROLL):
                spread[r * states:(r + 1) * states, :] = column(outs[count * states:(count + 1) * states, :], r)

            def settle_adjoints(group, slot):
                rows = pl.ds(pl.multiple_of(group * UNROLL, UNROLL), UNROLL)
                lamb[rows, lanes] = jnp.dot(inmap[rows, :], seen[slot], preferred_element_type=F32)
                total = lax.dot_general(drive[rows, lanes].astype(BF16), seen[slot], (((1,), (1,)), ((), ())),
                                        preferred_element_type=F32)
                bsum[rows, :] = total if g == 0 else bsum[rows, :] + total

            def retreat(group, adj, dsum, slot):
                base = pl.multiple_of(group * UNROLL, UNROLL)
                block = lane_block(outs, group - 1, states)
                for r in reversed(range(UNROLL)):
                    st = steps[pl.ds(base + r, 1), lanes]
                    sg = grads[pl.ds(base + r, 1), lanes]
                    at = pl.ds(pl.multiple_of((base + r) * states, states), states)
                    row = slice(r * states, (r + 1) * states)
                    lam = adj + widen(spread[row, :], width) * sg
                    spread[row, :] = column(block, r)
                    seen[slot, row, :] = lam.astype(BF16)
                    adj = fac[at, :] * lam
                    w = adj * hist[at, :]
                    dsum = dsum + w * st
                    q = w * decay
                    q = q[0:8] + q[8:16]
                    for k in range(width // 128):
                        turns[slot, k, r * 8:(r + 1) * 8, :] = q[:, k * 128:(k + 1) * 128]
                for k in range(width // 128):
                    for q in range(0, UNROLL, 8):
                        stepg[pl.ds(base + q, 8), g * width + k * 128:g * width + (k + 1) * 128] = tree(
                            [turns[slot, k, pl.ds(q * 8 + n, 8, stride=8), :] for n in range(8)])
                return adj, dsum

            def back_pair(i, carry):
                top = count - 1 - 2 * i
                settle_adjoints(top + 1, 1)
                carry = retreat(top, *carry, 0)
                settle_adjoints(top, 0)
                return retreat(top - 1, *carry, 1)

            adj, dsum = lax.fori_loop(0, count // 2, back_pair, (adjoint[:, lanes], jnp.zeros((states, width), F32)))
            settle_adjoints(0, 1)
            adjoint[:, lanes] = adj
            galog_ref[:, lanes] += dsum * decay
        xs = x_ref[...].astype(F32)
        sg = grads[...]
        lam_b = lamb[0:length, :]
        low = proj_ref[0:length, :].astype(BF16)
        pre = jnp.dot(low, dtw_ref[...], preferred_element_type=F32) + dtb_ref[...]
        pre_grad = (stepg[0:length, :] + xs * lam_b) * jax.nn.sigmoid(pre)
        gdtb_ref[...] += jnp.sum(pre_grad, axis=0, keepdims=True)
        gskip_ref[...] += jnp.sum(sg * xs, axis=0, keepdims=True)
        xg_ref[...] = (steps[...] * lam_b + skip_ref[...] * sg).astype(xg_ref.dtype)
        pre_low = pre_grad.astype(BF16)
        gdtw_ref[...] += lax.dot_general(low, pre_low, (((0,), (0,)), ((), ())), preferred_element_type=F32)
        pg_ref[0:length, :] = lax.dot_general(pre_low, dtw_ref[...], (((1,), (1,)), ((), ())), preferred_element_type=F32)
        mine = own_token(length, states)
        state = lax.broadcasted_iota(jnp.int32, (states, UNROLL * states), 1) % states
        pick = (state == lax.broadcasted_iota(jnp.int32, (states, UNROLL * states), 0)).astype(BF16)
        for row, sums in ((length, bsum[0:length, :]), (length + states, csum[UNROLL:UNROLL + length, :])):
            pg_ref[row:row + states, :] = lax.dot_general(
                pick, jnp.where(mine, sums, 0.0).astype(BF16), (((1,), (1,)), ((), ())), preferred_element_type=F32)


def scan_backward(order, lengths, proj, x, sg, starts, dtw, dtb, alog, skip, micro, micros, width=512):
    length, inner = x.shape
    count = length // CHUNK
    states = alog.shape[0]
    rank = dtw.shape[0]
    per_piece = count // order.shape[0]
    width = min(width, inner)
    rev = lambda cols: pl.BlockSpec((CHUNK, cols), lambda i, order, lengths: (count - 1 - i, 0))
    return pl.pallas_call(
        lambda *refs: scan_backward_kernel(*refs, width=width, micro=micro),
        grid_spec=pltpu.PrefetchScalarGridSpec(
            num_scalar_prefetch=2,
            grid=(count,),
            in_specs=[
                pl.BlockSpec((CHUNK + 2 * states, rank), lambda i, order, lengths: (count - 1 - i, 0)), rev(inner),
                pl.BlockSpec((CHUNK, inner), placed(per_piece, count, micro, micros, True)),
                pl.BlockSpec((1, states, inner), lambda i, order, lengths: (count - 1 - i, 0, 0)),
                whole_spec((rank, inner)), whole_spec((1, inner)), whole_spec((states, inner)), whole_spec((1, inner)),
            ],
            out_specs=[
                pl.BlockSpec((CHUNK + 2 * states, rank), lambda i, order, lengths: (count - 1 - i, 0)),
                rev(inner),
                whole_spec((rank, inner)), whole_spec((1, inner)), whole_spec((states, inner)), whole_spec((1, inner)),
            ],
            scratch_shapes=[
                pltpu.VMEM((states, inner), F32),
                pltpu.VMEM((CHUNK, inner), F32),
                pltpu.VMEM((CHUNK + UNROLL, inner), F32),
                pltpu.VMEM((CHUNK, inner), F32),
                pltpu.VMEM(((CHUNK // UNROLL + 2) * states, 128), F32),
                pltpu.VMEM(((CHUNK // UNROLL + 2) * states, 128), F32),
                pltpu.VMEM((CHUNK + UNROLL, UNROLL * states), BF16),
                pltpu.VMEM((UNROLL * states, 128), F32),
                pltpu.VMEM((2, UNROLL * states, width), BF16),
                pltpu.VMEM((2, width // 128, 8 * UNROLL, 128), F32),
                pltpu.VMEM((CHUNK * states, width), F32),
                pltpu.VMEM((CHUNK * states, width), F32),
                pltpu.VMEM((CHUNK + UNROLL, UNROLL * states), F32),
                pltpu.VMEM((CHUNK + UNROLL, UNROLL * states), F32),
                pltpu.VMEM((CHUNK + UNROLL, inner), F32),
                pltpu.VMEM((CHUNK + UNROLL, inner), F32),
            ],
        ),
        out_shape=[
            jax.ShapeDtypeStruct((count * (CHUNK + 2 * states), rank), F32),
            jax.ShapeDtypeStruct((length, inner), BF16),
            jax.ShapeDtypeStruct((rank, inner), F32),
            jax.ShapeDtypeStruct((1, inner), F32),
            jax.ShapeDtypeStruct((states, inner), F32),
            jax.ShapeDtypeStruct((1, inner), F32),
        ],
        name="scan_backward",
    )(order, lengths, proj, x, sg, starts, dtw, dtb, alog, skip)


def conv_forward_kernel(order, lengths, *refs, peers, micro):
    pieces = refs[:peers]
    gain_ref, wb_ref, cw_ref, cb_ref, xw_ref, held_ref, normed_ref, branch_ref, x_ref, proj_ref, pad = refs[peers:]
    length, inner = x_ref.shape
    at = pl.program_id(0)

    @pl.when(at == 0)
    def _():
        pad[0:8, :] = jnp.zeros((8, inner), F32)

    live = at * length < lengths[micro]

    @pl.when(jnp.logical_not(live))
    def _():
        for ref in (normed_ref, branch_ref, x_ref, proj_ref):
            ref[...] = jnp.zeros_like(ref)

    for p in range(peers):
        @pl.when(jnp.logical_and(live, order[at] == p))
        def _():
            tokens = pieces[p][...].astype(F32)
            scale = lax.rsqrt(jnp.mean(tokens * tokens, axis=-1, keepdims=True) + EPSILON)
            normed_ref[...] = (tokens * scale * gain_ref[...]).astype(BF16)

    @pl.when(live)
    def _():
        groups = wb_ref.shape[0]
        deep = normed_ref.shape[1] // groups
        branch = sum(jnp.dot(normed_ref[:, d * deep:(d + 1) * deep], wb_ref[d, 0:deep, :], preferred_element_type=F32)
                     for d in range(groups)).astype(BF16)
        branch_ref[...] = branch
        pad[8:8 + length, :] = branch.astype(F32)
        pre = cb_ref[...] + sum(cw_ref[k:k + 1, :] * pad[5 + k:5 + k + length, :] for k in range(KCONV))
        x = (pre * jax.nn.sigmoid(pre)).astype(BF16)
        x_ref[...] = x
        rank = proj_ref.shape[1]
        low = lax.dot_general(x, xw_ref[0:rank, :], (((1,), (1,)), ((), ())), preferred_element_type=F32)
        maps = lax.dot_general(xw_ref[rank:, :], x, (((1,), (1,)), ((), ())), preferred_element_type=F32)
        rows = CHUNK + maps.shape[0]
        for k in range(length // CHUNK):
            proj_ref[k * rows:k * rows + CHUNK, :] = low[k * CHUNK:(k + 1) * CHUNK, :]
            proj_ref[k * rows + CHUNK:(k + 1) * rows, :] = maps[:, k * CHUNK:(k + 1) * CHUNK]
        pad[0:8, :] = pad[length:length + 8, :]


def conv_forward(order, lengths, pieces, gain, wb, cw, cb, xw, rank, micro, micros, held):
    peers = len(pieces)
    tokens, width = pieces[0].shape
    inner = wb.shape[2]
    cols = xw.shape[0]
    rows = tokens // CHUNK * (CHUNK + cols - rank)
    first = held is None
    return pl.pallas_call(
        lambda *refs: conv_forward_kernel(*refs, peers=peers, micro=micro),
        grid_spec=pltpu.PrefetchScalarGridSpec(
            num_scalar_prefetch=2,
            grid=(peers,),
            in_specs=[whole_spec((tokens, width))] * peers + [
                whole_spec((1, width)),
                whole_spec(wb.shape), whole_spec((KCONV, inner)), whole_spec((1, inner)), whole_spec((cols, inner)),
                pl.BlockSpec(memory_space=pl.ANY),
            ],
            out_specs=[
                pl.BlockSpec((tokens, width), placed(1, peers, micro, micros)),
                spec_nat(tokens, inner), spec_nat(tokens, inner), spec_nat(rows, rank),
            ],
            scratch_shapes=[pltpu.VMEM((tokens + 8, inner), F32)],
        ),
        out_shape=[
            jax.ShapeDtypeStruct((micros * peers * tokens, width), BF16),
            jax.ShapeDtypeStruct((peers * tokens, inner), BF16),
            jax.ShapeDtypeStruct((peers * tokens, inner), BF16),
            jax.ShapeDtypeStruct((peers * rows, rank), F32),
        ],
        input_output_aliases={} if first else {peers + 7: 0},
        name="conv_forward",
    )(order, lengths, *pieces, gain, wb, cw, cb, xw, gain if first else held)


def conv_backward_kernel(order, lengths, pg_ref, xg_ref, branch_ref, prev_ref, x_ref, cw_ref, cb_ref, xw_ref, held_ref,
                         mixed_ref, gxw_ref, gcb_ref, gcw_ref, pad, ahead, *, micro):
    length, inner = x_ref.shape

    @pl.when(pl.program_id(0) == 0)
    def _():
        ahead[length:length + 8, :] = jnp.zeros((8, inner), F32)
        gxw_ref[...] = jnp.zeros_like(gxw_ref)
        gcb_ref[...] = jnp.zeros_like(gcb_ref)
        gcw_ref[...] = jnp.zeros_like(gcw_ref)

    at = pl.num_programs(0) - 1 - pl.program_id(0)
    live = at * length < lengths[micro]

    @pl.when(jnp.logical_not(live))
    def _():
        mixed_ref[...] = jnp.zeros_like(mixed_ref)

    @pl.when(live)
    def _():
        earliest = pl.program_id(0) == pl.num_programs(0) - 1
        pad[0:8, :] = jnp.where(earliest, 0.0, prev_ref[...].astype(F32)[8:16, :])
        pad[8:8 + length, :] = branch_ref[...].astype(F32)
        pre = cb_ref[...] + sum(cw_ref[k:k + 1, :] * pad[5 + k:5 + k + length, :] for k in range(KCONV))
        sig = jax.nn.sigmoid(pre)
        rank = pg_ref.shape[1]
        rows = CHUNK + xw_ref.shape[0] - rank
        low, maps = [], []
        for k in range(length // CHUNK):
            low.append(pg_ref[k * rows:k * rows + CHUNK, :].astype(BF16))
            maps.append(pg_ref[k * rows + CHUNK:(k + 1) * rows, :].astype(BF16))
        low, maps = jnp.concatenate(low, axis=0), jnp.concatenate(maps, axis=1)
        grad = (jnp.dot(low, xw_ref[0:rank, :], preferred_element_type=F32)
                + lax.dot_general(maps, xw_ref[rank:, :], (((0,), (0,)), ((), ())), preferred_element_type=F32)
                + xg_ref[...].astype(F32))
        grad = grad * (sig * (1.0 + pre * (1.0 - sig)))
        ahead[0:length, :] = grad
        gcb_ref[...] += jnp.sum(grad, axis=0, keepdims=True)
        for k in range(KCONV):
            gcw_ref[k:k + 1, :] += jnp.sum(grad * pad[5 + k:5 + k + length, :], axis=0, keepdims=True)
        mixed = sum(cw_ref[k:k + 1, :] * ahead[3 - k:3 - k + length, :] for k in range(KCONV))
        mixed_ref[...] = mixed.astype(BF16)
        gxw_ref[0:rank, :] += lax.dot_general(low, x_ref[...], (((0,), (0,)), ((), ())), preferred_element_type=F32)
        gxw_ref[rank:, :] += jnp.dot(maps, x_ref[...], preferred_element_type=F32)
        ahead[length:length + 8, :] = ahead[0:8, :]


def conv_backward(order, lengths, pg, xg, branch, x, cw, cb, xw, micro, micros, held):
    length, inner = x.shape
    tokens = length // order.shape[0]
    count = length // tokens
    cols = xw.shape[0]
    first = held is None
    rank = pg.shape[1]
    rows = pg.shape[0] // count
    rev = lambda width: pl.BlockSpec((tokens, width), lambda i, order, lengths: (count - 1 - i, 0))
    return pl.pallas_call(
        lambda *refs: conv_backward_kernel(*refs, micro=micro),
        grid_spec=pltpu.PrefetchScalarGridSpec(
            num_scalar_prefetch=2,
            grid=(count,),
            in_specs=[
                pl.BlockSpec((rows, rank), lambda i, order, lengths: (count - 1 - i, 0)), rev(inner), rev(inner),
                pl.BlockSpec((16, inner), lambda i, order, lengths: (jnp.maximum((count - 1 - i) * (tokens // 16) - 1, 0), 0)),
                rev(inner),
                whole_spec((KCONV, inner)), whole_spec((1, inner)), whole_spec((cols, inner)),
                pl.BlockSpec(memory_space=pl.ANY),
            ],
            out_specs=[
                pl.BlockSpec((tokens, inner), placed(1, count, micro, micros, True)),
                whole_spec((cols, inner)), whole_spec((1, inner)), whole_spec((KCONV, inner)),
            ],
            scratch_shapes=[pltpu.VMEM((tokens + 8, inner), F32), pltpu.VMEM((tokens + 8, inner), F32)],
        ),
        out_shape=[
            jax.ShapeDtypeStruct((micros * length, inner), BF16),
            jax.ShapeDtypeStruct((cols, inner), F32),
            jax.ShapeDtypeStruct((1, inner), F32),
            jax.ShapeDtypeStruct((KCONV, inner), F32),
        ],
        input_output_aliases={} if first else {10: 0},
        name="conv_backward",
    )(order, lengths, pg, xg, branch, branch, x, cw, cb, xw, cb if first else held)


def partner(value, step):
    peers = lax.axis_size("seq")
    return lax.ppermute(value, "seq", [(i, i ^ step) for i in range(peers)])


def halvings():
    step = lax.axis_size("seq") // 2
    while step >= 1:
        yield step
        step //= 2


def reversed_bits(value, peers):
    out = value * 0
    step = 1
    while step < peers:
        out = out * 2 + (value // step) % 2
        step *= 2
    return out


def finish_piece(value):
    for step in reversed(list(halvings())[:-1]):
        half = value.shape[0] // 2
        value = value[:half].astype(F32) + partner(value[half:], step).astype(F32)
        value = value if step == lax.axis_size("seq") // 2 else value.astype(BF16)
    return value


def sum_over_pieces(value):
    for step in reversed(list(halvings())[:-1]):
        value = value.astype(F32) + partner(value, step).astype(F32)
        value = value if step == lax.axis_size("seq") // 2 else value.astype(BF16)
    return value


def sum_to_owner(whole):
    ranks = lax.axis_size("dp")
    me = lax.axis_index("dp")
    share = whole.shape[1] // ranks
    parts = jnp.stack([lax.dynamic_slice_in_dim(whole, (me ^ r) * share, share, 1) for r in range(ranks)]).astype(F32)
    step = 1
    while parts.shape[0] > 1:
        parts = parts.reshape((parts.shape[0] // 2, 2) + parts.shape[1:])
        given = parts[:, 1].astype(BF16)
        other = lax.ppermute(given, "dp", [(i, i ^ step) for i in range(ranks)])
        parts = parts[:, 0] + other.astype(F32)
        step *= 2
    return parts[0]


def dot(left, right, dims, kind=F32):
    return lax.dot_general(left, right, (dims, ((), ())), preferred_element_type=kind)


def body(tokens, lengths, cotangent, norm_gain, in_weight, conv_weight, conv_bias, x_weight, dt_weight,
         dt_bias, a_log, skip_d, out_weight):
    micros, slots, piece, width = tokens.shape
    peers, groups = lax.axis_size("seq"), lax.axis_size("dp")
    me = lax.axis_index("seq")
    share = conv_bias.shape[0]
    inner = share * groups
    rows = in_weight.shape[0]
    rank = dt_weight.shape[0]
    states = a_log.shape[0]
    cols = x_weight.shape[1]
    length = piece * peers
    order = reversed_bits(jnp.arange(peers, dtype=jnp.int32) ^ me, peers)
    tokens, cotangent = tokens[:, 0], cotangent[:, 0]
    held = lengths[:, 0]

    gain_part = norm_gain
    for step in halvings():
        gain_part = jnp.concatenate([gain_part, partner(gain_part, step)])
    gain_part = gain_part.reshape(peers, rows)
    gain_part = jnp.concatenate([lax.dynamic_slice_in_dim(gain_part, order[q], 1) for q in range(peers)])
    gain_rows = peers * rows // share
    small = jnp.concatenate([
        a_log, conv_weight, conv_bias[None], dt_bias[None], skip_d[None], gain_part.reshape(gain_rows, share),
        jnp.zeros((states - KCONV - 3 - gain_rows, share), BF16), dt_weight, x_weight.T], axis=0)
    packed = small.shape[0]

    def mine(half):
        own = half.reshape(rows, groups, peers, share).transpose(2, 0, 1, 3).reshape(peers * rows, inner)
        return lax.all_to_all(own, "seq", split_axis=0, concat_axis=0, tiled=True)

    first = jnp.concatenate([mine(in_weight[:, :inner * peers]), small.reshape(-1, inner)], axis=0)
    first = lax.all_gather(first, "dp", axis=0, tiled=False)
    pieces = [[tokens[m]] for m in range(micros)]
    for step in halvings():
        for m in range(micros):
            pieces[m] = pieces[m] + [partner(part, step) for part in pieces[m]]
    late, pieces = lax.optimization_barrier((in_weight[:, inner * peers:], pieces))
    wg = lax.all_gather(mine(late), "dp", axis=0, tiled=True)
    wo = lax.all_gather(out_weight, "dp", axis=0, tiled=True)
    small = first[:, peers * rows:].reshape(groups, packed, share)
    at = states + KCONV + 3
    gain = small[:, at:at + gain_rows].reshape(1, width).astype(F32)
    small = jnp.concatenate([small[d] for d in range(groups)], axis=1)
    alog = small[0:states]
    at = states
    cw = small[at:at + KCONV].astype(F32)
    cb = small[at + KCONV:at + KCONV + 1].astype(F32)
    dtb = small[at + KCONV + 1:at + KCONV + 2].astype(F32)
    skip = small[at + KCONV + 2:at + KCONV + 3].astype(F32)
    dtw = small[2 * states:2 * states + rank]
    xw = small[2 * states + rank:]

    positions = me * piece + jnp.arange(piece, dtype=jnp.int32)
    valid = (positions[None, :] < lengths).astype(F32)[..., None]
    own_grad = (valid * cotangent.astype(F32)).astype(BF16)
    own_grad, pieces = lax.optimization_barrier((own_grad, pieces))
    grads = [own_grad]
    for step in list(halvings())[:-1]:
        grads = grads + [partner(part, step) for part in grads]
    convs, normed = [], None
    for m in range(micros):
        normed, branch, x, proj = conv_forward(order, held, pieces[m], gain, first, cw, cb, xw, rank, m, micros, normed)
        proj = (proj + partner(proj, 1)).astype(BF16)
        if m + 1 < micros:
            proj, pieces[m + 1], grads = lax.optimization_barrier((proj, pieces[m + 1], grads))
        convs.append((branch, x, sum_over_pieces(proj)))
    grads = grads + [partner(part, 1) for part in grads]
    y, starts = None, []
    for m in range(micros):
        y, start = scan_forward(order, held, convs[m][2], convs[m][1], dtw, dtb, alog, skip, m, micros, y)
        starts.append(start)
    normed, y = lax.optimization_barrier((normed, y))
    gate = dot(normed, wg, ((1,), (0,)))
    sig = jax.nn.sigmoid(gate)
    yf = y.astype(F32)
    gated = (yf * gate * sig).astype(BF16)
    out_grad = jnp.concatenate(grads, axis=0).reshape(micros * length, width)
    gwo = dot(gated, out_grad, ((0,), (0,)), BF16)
    gwo, gated, out_grad = lax.optimization_barrier((gwo, gated, out_grad))
    gg = dot(out_grad, wo, ((1,), (1,)))
    sg = (gg * gate * sig).astype(BF16)
    gate_grad = (gg * yf * sig * (1.0 + gate * (1.0 - sig))).astype(BF16)
    half = micros * length // 2
    given = dot(gated[half:], wo, ((1,), (0,)), BF16)
    kept = dot(gated[:half], wo, ((1,), (0,)), BF16)
    given, kept, gate_grad = lax.optimization_barrier((given, kept, gate_grad))
    gwg = dot(normed, gate_grad, ((0,), (0,)), BF16)
    added = (kept.astype(F32) + partner(given, 1).astype(F32)).astype(BF16)
    gwg, sg, added = lax.optimization_barrier((gwg, sg, added))
    added = finish_piece(added)
    gwo = lax.psum_scatter(gwo, "dp", scatter_dimension=0, tiled=True)
    gwg = lax.psum_scatter(gwg, "dp", scatter_dimension=0, tiled=True)
    gwg = lax.all_to_all(gwg, "seq", split_axis=0, concat_axis=0, tiled=True)
    backs = []
    for m in range(micros):
        given = sg
        if m == micros - 1:
            given, gwo, added = lax.optimization_barrier((given, gwo, added))
            result = (valid * (tokens.astype(F32) + added.reshape(micros, piece, width))).astype(BF16)
        backs.append(list(scan_backward(
            order, held, convs[m][2], convs[m][1], given, starts[m], dtw, dtb, alog, skip, m, micros)))
        backs[m][0] = (backs[m][0] + partner(backs[m][0], 1)).astype(BF16)
        if m + 1 < micros:
            backs[m][0] = sum_over_pieces(backs[m][0])
    for m in range(micros - 1):
        backs[m][0], backs[-1][1] = lax.optimization_barrier((backs[m][0], backs[-1][1]))
    mixed, totals = None, None
    for m in range(micros):
        pg, xg, gdtw, gdtb, galog, gskip = backs[m]
        if m == micros - 1:
            pg, mixed, gate_grad = lax.optimization_barrier((pg, mixed, gate_grad))
            pg = sum_over_pieces(pg)
            early = dot(gate_grad, wg, ((1,), (1,)))
            pg, early = lax.optimization_barrier((pg, early))
        mixed, gxw, gcb, gcw = conv_backward(
            order, held, pg, xg, convs[m][0], convs[m][1], cw, cb, xw, m, micros, mixed)
        part = [galog, gcw, gcb, gdtb, gskip, gdtw, gxw]
        totals = part if totals is None else [a + b for a, b in zip(totals, part)]
    gwb = dot(normed, mixed, ((0,), (0,)), BF16)
    gwb, totals, mixed = lax.optimization_barrier((gwb, totals, mixed))
    gwb = lax.psum_scatter(gwb, "dp", scatter_dimension=0, tiled=True)
    gsmall = sum_to_owner(jnp.concatenate(totals, axis=0))
    wb = first[:, :peers * rows].reshape(width, inner)
    w = (early + dot(mixed, wb, ((1,), (1,)))).astype(BF16)
    w = finish_piece((w[:half].astype(F32) + partner(w[half:], 1).astype(F32)).astype(BF16)).reshape(micros, piece, width)
    w, gwb, gsmall, gwg = lax.optimization_barrier((w, gwb, gsmall, gwg))
    w = w * gain
    inputs = tokens.astype(F32)
    scale = lax.rsqrt(jnp.mean(inputs * inputs, axis=-1, keepdims=True) + EPSILON)
    input_grad = (own_grad.astype(F32) + scale * w - inputs * (scale * scale * scale)
                  * jnp.mean(w * inputs, axis=-1, keepdims=True)).astype(BF16)
    gwb = lax.all_to_all(gwb, "seq", split_axis=0, concat_axis=0, tiled=True)
    spread = lambda g: g.astype(F32).reshape(peers, rows, groups, share).transpose(1, 2, 0, 3).reshape(rows, inner * peers)
    total = jnp.concatenate([spread(gwb), spread(gwg)], axis=1)
    g_gain = jnp.sum(in_weight.astype(F32) * total, axis=1) / norm_gain.astype(F32)
    pieces, at = [], 0
    for count in (states, KCONV, 1, 1, 1, rank, cols):
        pieces.append(gsmall[at:at + count])
        at += count
    galog, gcw, gcb, gdtb, gskip, gdtw, gxw = pieces
    return (
        result[:, None], input_grad[:, None], g_gain, total, gcw, gcb[0], gxw.T, gdtw, gdtb[0], galog, gskip[0],
        gwo.astype(F32),
    )


def solution(mesh):
    placed = (
        P(None, "dp", "seq", None),
        P(None, "dp"),
        P(None, "dp", "seq", None),
        P(("dp", "seq")),
        P(("dp", "seq"), None),
        P(None, ("dp", "seq")),
        P(("dp", "seq")),
        P(("dp", "seq"), None),
        P(None, ("dp", "seq")),
        P(("dp", "seq")),
        P(None, ("dp", "seq")),
        P(("dp", "seq")),
        P(("dp", "seq"), None),
    )
    return jax.shard_map(
        body,
        mesh=mesh,
        in_specs=placed,
        out_specs=(
            P(None, "dp", "seq", None),
            P(None, "dp", "seq", None),
            P(("dp", "seq")),
            P(("dp", "seq"), None),
            P(None, ("dp", "seq")),
            P(("dp", "seq")),
            P(("dp", "seq"), None),
            P(None, ("dp", "seq")),
            P(("dp", "seq")),
            P(None, ("dp", "seq")),
            P(("dp", "seq")),
            P(("dp", "seq"), None),
        ),
        check_vma=False,
    )
```

```python
import jax
import jax.numpy as jnp
from jax import lax
from jax.experimental import pallas as pl
from jax.experimental.pallas import tpu as pltpu
from jax.sharding import PartitionSpec as P

F32 = jnp.float32
BF16 = jnp.bfloat16
LOG2E = 1.4426950408889634
CHUNK = 128
KCONV = 4
EPSILON = 1e-05
UNROLL = 16


def softplus(v):
    e = jnp.exp(-jnp.abs(v))
    series = e * (1.0 + e * (-0.5 + e * (1.0 / 3.0 - 0.25 * e)))
    return jnp.maximum(v, 0.0) + jnp.where(e < 0.0078125, series, jnp.log(1.0 + e))


def tree(values):
    while len(values) > 1:
        values = [a + b for a, b in zip(values[0::2], values[1::2])]
    return values[0]


def widen(value, width):
    return jnp.concatenate([value] * (width // 128), axis=1) if width > 128 else value


def own_token(tokens, states):
    row = lax.broadcasted_iota(jnp.int32, (tokens, UNROLL * states), 0) % UNROLL
    return row == lax.broadcasted_iota(jnp.int32, (tokens, UNROLL * states), 1) // states


def diagonal(maps):
    states, tokens = maps.shape
    column = lax.broadcasted_iota(jnp.int32, (states, UNROLL * states), 1) % states
    repeat = (column == lax.broadcasted_iota(jnp.int32, (states, UNROLL * states), 0)).astype(BF16)
    every = lax.dot_general(maps.astype(BF16), repeat, (((0,), (0,)), ((), ())), preferred_element_type=F32)
    return jnp.where(own_token(tokens, states), every, 0.0).astype(BF16)


def stagger(maps, out):
    states, tokens = maps.shape
    for i in range(tokens // UNROLL):
        at = (i + 1) * states
        out[at:at + states, :] = maps if i == 0 else pltpu.roll(maps, tokens - i * UNROLL, 1)


def lane_block(maps, group, states):
    return maps[pl.ds(pl.multiple_of((group + 1) * states, states), states), :]


def column(block, r):
    return jnp.broadcast_to(block[:, r:r + 1], (block.shape[0], 128))


def scan_forward_kernel(order, lengths, proj_ref, x_ref, dtw_ref, dtb_ref, alog_ref, skip_ref, held_ref,
                        y_ref, start_ref, state, steps, drive, ins, outs, spread, seen, ysum, *, width, micro):
    length, inner = x_ref.shape
    states = state.shape[0]
    live = pl.program_id(0) * length < lengths[micro]

    @pl.when(pl.program_id(0) == 0)
    def _():
        state[...] = jnp.zeros_like(state)

    @pl.when(jnp.logical_not(live))
    def _():
        y_ref[...] = jnp.zeros_like(y_ref)
        start_ref[...] = jnp.zeros_like(start_ref)

    @pl.when(live)
    def _():
        start_ref[0] = state[...]
        xs = x_ref[...].astype(F32)
        pre = jnp.dot(proj_ref[0:length, :].astype(BF16), dtw_ref[...], preferred_element_type=F32) + dtb_ref[...]
        step = softplus(pre)
        steps[...] = step
        drive[...] = step * xs
        stagger(proj_ref[length:length + states, :], ins)
        outs[UNROLL:UNROLL + length, :] = diagonal(proj_ref[length + states:length + 2 * states, :])
        for g in range(inner // width):
            lanes = slice(g * width, (g + 1) * width)
            rate = -jnp.exp(alog_ref[:, lanes].astype(F32)) * LOG2E
            for r in range(UNROLL):
                spread[r * states:(r + 1) * states, :] = column(ins[states:2 * states, :], r)

            def settle(group, slot):
                rows = pl.ds(pl.multiple_of(group * UNROLL, UNROLL), UNROLL)
                ysum[rows, lanes] = jnp.dot(outs[rows, :], seen[slot], preferred_element_type=F32)

            def advance(group, h, slot):
                base = pl.multiple_of(group * UNROLL, UNROLL)
                block = lane_block(ins, group + 1, states)
                for r in range(UNROLL):
                    st = steps[pl.ds(base + r, 1), lanes]
                    dr = drive[pl.ds(base + r, 1), lanes]
                    row = slice(r * states, (r + 1) * states)
                    h = jnp.exp2(st * rate) * h + widen(spread[row, :], width) * dr
                    spread[row, :] = column(block, r)
                    seen[slot, row, :] = h.astype(BF16)
                return h

            def pair(i, h):
                settle(2 * i, 1)
                h = advance(2 * i, h, 0)
                settle(2 * i + 1, 0)
                return advance(2 * i + 1, h, 1)

            state[:, lanes] = lax.fori_loop(0, length // UNROLL // 2, pair, state[:, lanes])
            settle(length // UNROLL, 1)
        y_ref[...] = (ysum[UNROLL:UNROLL + length, :] + skip_ref[...] * xs).astype(y_ref.dtype)


def spec_nat(length, cols):
    return pl.BlockSpec((length, cols), lambda i, order, lengths: (i, 0))


def whole_spec(shape):
    return pl.BlockSpec(shape, lambda i, order, lengths: (0,) * len(shape))


def placed(per_piece, count, micro, micros, reverse=False):
    def index(i, order, lengths):
        at = count - 1 - i if reverse else i
        return ((order[at // per_piece] * micros + micro) * per_piece + at % per_piece, 0)
    return index


def scan_forward(order, lengths, proj, x, dtw, dtb, alog, skip, micro, micros, held, width=512):
    length, inner = x.shape
    count = length // CHUNK
    states = alog.shape[0]
    rank = dtw.shape[0]
    per_piece = count // order.shape[0]
    width = min(width, inner)
    first = held is None
    return pl.pallas_call(
        lambda *refs: scan_forward_kernel(*refs, width=width, micro=micro),
        grid_spec=pltpu.PrefetchScalarGridSpec(
            num_scalar_prefetch=2,
            grid=(count,),
            in_specs=[
                spec_nat(CHUNK + 2 * states, rank), spec_nat(CHUNK, inner),
                whole_spec((rank, inner)), whole_spec((1, inner)), whole_spec((states, inner)), whole_spec((1, inner)),
                pl.BlockSpec(memory_space=pl.ANY),
            ],
            out_specs=[
                pl.BlockSpec((CHUNK, inner), placed(per_piece, count, micro, micros)),
                pl.BlockSpec((1, states, inner), lambda i, order, lengths: (i, 0, 0)),
            ],
            scratch_shapes=[
                pltpu.VMEM((states, inner), F32),
                pltpu.VMEM((CHUNK, inner), F32),
                pltpu.VMEM((CHUNK, inner), F32),
                pltpu.VMEM(((CHUNK // UNROLL + 2) * states, 128), F32),
                pltpu.VMEM((CHUNK + UNROLL, UNROLL * states), BF16),
                pltpu.VMEM((UNROLL * states, 128), F32),
                pltpu.VMEM((2, UNROLL * states, width), BF16),
                pltpu.VMEM((CHUNK + UNROLL, inner), F32),
            ],
        ),
        out_shape=[
            jax.ShapeDtypeStruct((micros * length, inner), BF16),
            jax.ShapeDtypeStruct((count, states, inner), F32),
        ],
        input_output_aliases={} if first else {8: 0},
        name="scan_forward",
    )(order, lengths, proj, x, dtw, dtb, alog, skip, dtb if first else held)


def scan_backward_kernel(order, lengths, proj_ref, x_ref, sg_ref, start_ref, dtw_ref, dtb_ref, alog_ref, skip_ref,
                         pg_ref, xg_ref, gdtw_ref, gdtb_ref, galog_ref, gskip_ref,
                         adjoint, steps, drive, grads, ins, outs, inmap, spread, seen, turns, hist, fac, bsum, csum,
                         lamb, stepg, *,
                         width, micro):
    length, inner = x_ref.shape
    states = adjoint.shape[0]
    at = pl.num_programs(0) - 1 - pl.program_id(0)
    live = at * length < lengths[micro]

    @pl.when(pl.program_id(0) == 0)
    def _():
        adjoint[...] = jnp.zeros_like(adjoint)
        gdtw_ref[...] = jnp.zeros_like(gdtw_ref)
        gdtb_ref[...] = jnp.zeros_like(gdtb_ref)
        galog_ref[...] = jnp.zeros_like(galog_ref)
        gskip_ref[...] = jnp.zeros_like(gskip_ref)

    @pl.when(jnp.logical_not(live))
    def _():
        pg_ref[...] = jnp.zeros_like(pg_ref)
        xg_ref[...] = jnp.zeros_like(xg_ref)

    @pl.when(live)
    def _():
        low = proj_ref[0:length, :].astype(BF16)
        pre = jnp.dot(low, dtw_ref[...], preferred_element_type=F32) + dtb_ref[...]
        step = softplus(pre)
        steps[...] = step
        drive[0:length, :] = step * x_ref[...].astype(F32)
        grads[...] = sg_ref[...].astype(F32)
        stagger(proj_ref[length:length + states, :], ins)
        stagger(proj_ref[length + states:length + 2 * states, :], outs)
        inmap[0:length, :] = diagonal(proj_ref[length:length + states, :])
        count = length // UNROLL
        for g in range(inner // width):
            lanes = slice(g * width, (g + 1) * width)
            decay = -jnp.exp(alog_ref[:, lanes].astype(F32))
            rate = decay * LOG2E
            for r in range(UNROLL):
                spread[r * states:(r + 1) * states, :] = column(ins[states:2 * states, :], r)

            def settle_states(group, slot):
                given = pl.ds(pl.multiple_of(jnp.maximum(group - 1, 0) * UNROLL, UNROLL), UNROLL)
                rows = pl.ds(pl.multiple_of(group * UNROLL, UNROLL), UNROLL)
                total = lax.dot_general(sg_ref[given, lanes], seen[slot], (((1,), (1,)), ((), ())),
                                        preferred_element_type=F32)
                csum[rows, :] = total if g == 0 else csum[rows, :] + total

            def advance(group, h, slot):
                base = pl.multiple_of(group * UNROLL, UNROLL)
                block = lane_block(ins, group + 1, states)
                for r in range(UNROLL):
                    st = steps[pl.ds(base + r, 1), lanes]
                    dr = drive[pl.ds(base + r, 1), lanes]
                    at = pl.ds(pl.multiple_of((base + r) * states, states), states)
                    row = slice(r * states, (r + 1) * states)
                    hist[at, :] = h
                    a = jnp.exp2(st * rate)
                    fac[at, :] = a
                    h = a * h + widen(spread[row, :], width) * dr
                    spread[row, :] = column(block, r)
                    seen[slot, row, :] = h.astype(BF16)
                return h

            def pair(i, h):
                settle_states(2 * i, 1)
                h = advance(2 * i, h, 0)
                settle_states(2 * i + 1, 0)
                return advance(2 * i + 1, h, 1)

            lax.fori_loop(0, count // 2, pair, start_ref[0, :, lanes])
            settle_states(count, 1)
            for r in range(UNROLL):
                spread[r * states:(r + 1) * states, :] = column(outs[count * states:(count + 1) * states, :], r)

            def settle_adjoints(group, slot):
                rows = pl.ds(pl.multiple_of(group * UNROLL, UNROLL), UNROLL)
                lamb[rows, lanes] = jnp.dot(inmap[rows, :], seen[slot], preferred_element_type=F32)
                total = lax.dot_general(drive[rows, lanes].astype(BF16), seen[slot], (((1,), (1,)), ((), ())),
                                        preferred_element_type=F32)
                bsum[rows, :] = total if g == 0 else bsum[rows, :] + total

            def retreat(group, adj, dsum, slot):
                base = pl.multiple_of(group * UNROLL, UNROLL)
                block = lane_block(outs, group - 1, states)
                for r in reversed(range(UNROLL)):
                    st = steps[pl.ds(base + r, 1), lanes]
                    sg = grads[pl.ds(base + r, 1), lanes]
                    at = pl.ds(pl.multiple_of((base + r) * states, states), states)
                    row = slice(r * states, (r + 1) * states)
                    lam = adj + widen(spread[row, :], width) * sg
                    spread[row, :] = column(block, r)
                    seen[slot, row, :] = lam.astype(BF16)
                    adj = fac[at, :] * lam
                    w = adj * hist[at, :]
                    dsum = dsum + w * st
                    q = w * decay
                    q = q[0:8] + q[8:16]
                    for k in range(width // 128):
                        turns[slot, k, r * 8:(r + 1) * 8, :] = q[:, k * 128:(k + 1) * 128]
                for k in range(width // 128):
                    for q in range(0, UNROLL, 8):
                        stepg[pl.ds(base + q, 8), g * width + k * 128:g * width + (k + 1) * 128] = tree(
                            [turns[slot, k, pl.ds(q * 8 + n, 8, stride=8), :] for n in range(8)])
                return adj, dsum

            def back_pair(i, carry):
                top = count - 1 - 2 * i
                settle_adjoints(top + 1, 1)
                carry = retreat(top, *carry, 0)
                settle_adjoints(top, 0)
                return retreat(top - 1, *carry, 1)

            adj, dsum = lax.fori_loop(0, count // 2, back_pair, (adjoint[:, lanes], jnp.zeros((states, width), F32)))
            settle_adjoints(0, 1)
            adjoint[:, lanes] = adj
            galog_ref[:, lanes] += dsum * decay
        xs = x_ref[...].astype(F32)
        sg = grads[...]
        lam_b = lamb[0:length, :]
        low = proj_ref[0:length, :].astype(BF16)
        pre = jnp.dot(low, dtw_ref[...], preferred_element_type=F32) + dtb_ref[...]
        pre_grad = (stepg[0:length, :] + xs * lam_b) * jax.nn.sigmoid(pre)
        gdtb_ref[...] += jnp.sum(pre_grad, axis=0, keepdims=True)
        gskip_ref[...] += jnp.sum(sg * xs, axis=0, keepdims=True)
        xg_ref[...] = (steps[...] * lam_b + skip_ref[...] * sg).astype(xg_ref.dtype)
        pre_low = pre_grad.astype(BF16)
        gdtw_ref[...] += lax.dot_general(low, pre_low, (((0,), (0,)), ((), ())), preferred_element_type=F32)
        pg_ref[0:length, :] = lax.dot_general(pre_low, dtw_ref[...], (((1,), (1,)), ((), ())), preferred_element_type=F32)
        mine = own_token(length, states)
        state = lax.broadcasted_iota(jnp.int32, (states, UNROLL * states), 1) % states
        pick = (state == lax.broadcasted_iota(jnp.int32, (states, UNROLL * states), 0)).astype(BF16)
        for row, sums in ((length, bsum[0:length, :]), (length + states, csum[UNROLL:UNROLL + length, :])):
            pg_ref[row:row + states, :] = lax.dot_general(
                pick, jnp.where(mine, sums, 0.0).astype(BF16), (((1,), (1,)), ((), ())), preferred_element_type=F32)


def scan_backward(order, lengths, proj, x, sg, starts, dtw, dtb, alog, skip, micro, micros, width=512):
    length, inner = x.shape
    count = length // CHUNK
    states = alog.shape[0]
    rank = dtw.shape[0]
    per_piece = count // order.shape[0]
    width = min(width, inner)
    rev = lambda cols: pl.BlockSpec((CHUNK, cols), lambda i, order, lengths: (count - 1 - i, 0))
    return pl.pallas_call(
        lambda *refs: scan_backward_kernel(*refs, width=width, micro=micro),
        grid_spec=pltpu.PrefetchScalarGridSpec(
            num_scalar_prefetch=2,
            grid=(count,),
            in_specs=[
                pl.BlockSpec((CHUNK + 2 * states, rank), lambda i, order, lengths: (count - 1 - i, 0)), rev(inner),
                pl.BlockSpec((CHUNK, inner), placed(per_piece, count, micro, micros, True)),
                pl.BlockSpec((1, states, inner), lambda i, order, lengths: (count - 1 - i, 0, 0)),
                whole_spec((rank, inner)), whole_spec((1, inner)), whole_spec((states, inner)), whole_spec((1, inner)),
            ],
            out_specs=[
                pl.BlockSpec((CHUNK + 2 * states, rank), lambda i, order, lengths: (count - 1 - i, 0)),
                rev(inner),
                whole_spec((rank, inner)), whole_spec((1, inner)), whole_spec((states, inner)), whole_spec((1, inner)),
            ],
            scratch_shapes=[
                pltpu.VMEM((states, inner), F32),
                pltpu.VMEM((CHUNK, inner), F32),
                pltpu.VMEM((CHUNK + UNROLL, inner), F32),
                pltpu.VMEM((CHUNK, inner), F32),
                pltpu.VMEM(((CHUNK // UNROLL + 2) * states, 128), F32),
                pltpu.VMEM(((CHUNK // UNROLL + 2) * states, 128), F32),
                pltpu.VMEM((CHUNK + UNROLL, UNROLL * states), BF16),
                pltpu.VMEM((UNROLL * states, 128), F32),
                pltpu.VMEM((2, UNROLL * states, width), BF16),
                pltpu.VMEM((2, width // 128, 8 * UNROLL, 128), F32),
                pltpu.VMEM((CHUNK * states, width), F32),
                pltpu.VMEM((CHUNK * states, width), F32),
                pltpu.VMEM((CHUNK + UNROLL, UNROLL * states), F32),
                pltpu.VMEM((CHUNK + UNROLL, UNROLL * states), F32),
                pltpu.VMEM((CHUNK + UNROLL, inner), F32),
                pltpu.VMEM((CHUNK + UNROLL, inner), F32),
            ],
        ),
        out_shape=[
            jax.ShapeDtypeStruct((count * (CHUNK + 2 * states), rank), F32),
            jax.ShapeDtypeStruct((length, inner), BF16),
            jax.ShapeDtypeStruct((rank, inner), F32),
            jax.ShapeDtypeStruct((1, inner), F32),
            jax.ShapeDtypeStruct((states, inner), F32),
            jax.ShapeDtypeStruct((1, inner), F32),
        ],
        name="scan_backward",
    )(order, lengths, proj, x, sg, starts, dtw, dtb, alog, skip)


def conv_forward_kernel(order, lengths, *refs, peers, micro):
    pieces = refs[:peers]
    gain_ref, wb_ref, cw_ref, cb_ref, xw_ref, held_ref, normed_ref, branch_ref, x_ref, proj_ref, pad = refs[peers:]
    length, inner = x_ref.shape
    at = pl.program_id(0)

    @pl.when(at == 0)
    def _():
        pad[0:8, :] = jnp.zeros((8, inner), F32)

    live = at * length < lengths[micro]

    @pl.when(jnp.logical_not(live))
    def _():
        for ref in (normed_ref, branch_ref, x_ref, proj_ref):
            ref[...] = jnp.zeros_like(ref)

    for p in range(peers):
        @pl.when(jnp.logical_and(live, order[at] == p))
        def _():
            tokens = pieces[p][...].astype(F32)
            scale = lax.rsqrt(jnp.mean(tokens * tokens, axis=-1, keepdims=True) + EPSILON)
            normed_ref[...] = (tokens * scale * gain_ref[...]).astype(BF16)

    @pl.when(live)
    def _():
        branch = jnp.dot(normed_ref[...], wb_ref[...], preferred_element_type=F32).astype(BF16)
        branch_ref[...] = branch
        pad[8:8 + length, :] = branch.astype(F32)
        pre = cb_ref[...] + sum(cw_ref[k:k + 1, :] * pad[5 + k:5 + k + length, :] for k in range(KCONV))
        x = (pre * jax.nn.sigmoid(pre)).astype(BF16)
        x_ref[...] = x
        rank = proj_ref.shape[1]
        low = lax.dot_general(x, xw_ref[0:rank, :], (((1,), (1,)), ((), ())), preferred_element_type=F32)
        maps = lax.dot_general(xw_ref[rank:, :], x, (((1,), (1,)), ((), ())), preferred_element_type=F32)
        rows = CHUNK + maps.shape[0]
        for k in range(length // CHUNK):
            proj_ref[k * rows:k * rows + CHUNK, :] = low[k * CHUNK:(k + 1) * CHUNK, :]
            proj_ref[k * rows + CHUNK:(k + 1) * rows, :] = maps[:, k * CHUNK:(k + 1) * CHUNK]
        pad[0:8, :] = pad[length:length + 8, :]


def conv_forward(order, lengths, pieces, gain, wb, cw, cb, xw, rank, micro, micros, held):
    peers = len(pieces)
    tokens, width = pieces[0].shape
    inner = wb.shape[1]
    cols = xw.shape[0]
    rows = tokens // CHUNK * (CHUNK + cols - rank)
    first = held is None
    return pl.pallas_call(
        lambda *refs: conv_forward_kernel(*refs, peers=peers, micro=micro),
        grid_spec=pltpu.PrefetchScalarGridSpec(
            num_scalar_prefetch=2,
            grid=(peers,),
            in_specs=[whole_spec((tokens, width))] * peers + [
                whole_spec((1, width)),
                whole_spec(wb.shape), whole_spec((KCONV, inner)), whole_spec((1, inner)), whole_spec((cols, inner)),
                pl.BlockSpec(memory_space=pl.ANY),
            ],
            out_specs=[
                pl.BlockSpec((tokens, width), placed(1, peers, micro, micros)),
                spec_nat(tokens, inner), spec_nat(tokens, inner), spec_nat(rows, rank),
            ],
            scratch_shapes=[pltpu.VMEM((tokens + 8, inner), F32)],
        ),
        out_shape=[
            jax.ShapeDtypeStruct((micros * peers * tokens, width), BF16),
            jax.ShapeDtypeStruct((peers * tokens, inner), BF16),
            jax.ShapeDtypeStruct((peers * tokens, inner), BF16),
            jax.ShapeDtypeStruct((peers * rows, rank), F32),
        ],
        input_output_aliases={} if first else {peers + 7: 0},
        name="conv_forward",
    )(order, lengths, *pieces, gain, wb, cw, cb, xw, gain if first else held)


def conv_backward_kernel(order, lengths, pg_ref, xg_ref, branch_ref, prev_ref, x_ref, cw_ref, cb_ref, xw_ref, held_ref,
                         mixed_ref, gxw_ref, gcb_ref, gcw_ref, pad, ahead, *, micro):
    length, inner = x_ref.shape

    @pl.when(pl.program_id(0) == 0)
    def _():
        ahead[length:length + 8, :] = jnp.zeros((8, inner), F32)
        gxw_ref[...] = jnp.zeros_like(gxw_ref)
        gcb_ref[...] = jnp.zeros_like(gcb_ref)
        gcw_ref[...] = jnp.zeros_like(gcw_ref)

    at = pl.num_programs(0) - 1 - pl.program_id(0)
    live = at * length < lengths[micro]

    @pl.when(jnp.logical_not(live))
    def _():
        mixed_ref[...] = jnp.zeros_like(mixed_ref)

    @pl.when(live)
    def _():
        earliest = pl.program_id(0) == pl.num_programs(0) - 1
        pad[0:8, :] = jnp.where(earliest, 0.0, prev_ref[...].astype(F32)[8:16, :])
        pad[8:8 + length, :] = branch_ref[...].astype(F32)
        pre = cb_ref[...] + sum(cw_ref[k:k + 1, :] * pad[5 + k:5 + k + length, :] for k in range(KCONV))
        sig = jax.nn.sigmoid(pre)
        rank = pg_ref.shape[1]
        rows = CHUNK + xw_ref.shape[0] - rank
        low, maps = [], []
        for k in range(length // CHUNK):
            low.append(pg_ref[k * rows:k * rows + CHUNK, :].astype(BF16))
            maps.append(pg_ref[k * rows + CHUNK:(k + 1) * rows, :].astype(BF16))
        low, maps = jnp.concatenate(low, axis=0), jnp.concatenate(maps, axis=1)
        grad = (jnp.dot(low, xw_ref[0:rank, :], preferred_element_type=F32)
                + lax.dot_general(maps, xw_ref[rank:, :], (((0,), (0,)), ((), ())), preferred_element_type=F32)
                + xg_ref[...].astype(F32))
        grad = grad * (sig * (1.0 + pre * (1.0 - sig)))
        ahead[0:length, :] = grad
        gcb_ref[...] += jnp.sum(grad, axis=0, keepdims=True)
        for k in range(KCONV):
            gcw_ref[k:k + 1, :] += jnp.sum(grad * pad[5 + k:5 + k + length, :], axis=0, keepdims=True)
        mixed = sum(cw_ref[k:k + 1, :] * ahead[3 - k:3 - k + length, :] for k in range(KCONV))
        mixed_ref[...] = mixed.astype(BF16)
        gxw_ref[0:rank, :] += lax.dot_general(low, x_ref[...], (((0,), (0,)), ((), ())), preferred_element_type=F32)
        gxw_ref[rank:, :] += jnp.dot(maps, x_ref[...], preferred_element_type=F32)
        ahead[length:length + 8, :] = ahead[0:8, :]


def conv_backward(order, lengths, pg, xg, branch, x, cw, cb, xw, micro, micros, held):
    length, inner = x.shape
    tokens = length // order.shape[0]
    count = length // tokens
    cols = xw.shape[0]
    first = held is None
    rank = pg.shape[1]
    rows = pg.shape[0] // count
    rev = lambda width: pl.BlockSpec((tokens, width), lambda i, order, lengths: (count - 1 - i, 0))
    return pl.pallas_call(
        lambda *refs: conv_backward_kernel(*refs, micro=micro),
        grid_spec=pltpu.PrefetchScalarGridSpec(
            num_scalar_prefetch=2,
            grid=(count,),
            in_specs=[
                pl.BlockSpec((rows, rank), lambda i, order, lengths: (count - 1 - i, 0)), rev(inner), rev(inner),
                pl.BlockSpec((16, inner), lambda i, order, lengths: (jnp.maximum((count - 1 - i) * (tokens // 16) - 1, 0), 0)),
                rev(inner),
                whole_spec((KCONV, inner)), whole_spec((1, inner)), whole_spec((cols, inner)),
                pl.BlockSpec(memory_space=pl.ANY),
            ],
            out_specs=[
                pl.BlockSpec((tokens, inner), placed(1, count, micro, micros, True)),
                whole_spec((cols, inner)), whole_spec((1, inner)), whole_spec((KCONV, inner)),
            ],
            scratch_shapes=[pltpu.VMEM((tokens + 8, inner), F32), pltpu.VMEM((tokens + 8, inner), F32)],
        ),
        out_shape=[
            jax.ShapeDtypeStruct((micros * length, inner), BF16),
            jax.ShapeDtypeStruct((cols, inner), F32),
            jax.ShapeDtypeStruct((1, inner), F32),
            jax.ShapeDtypeStruct((KCONV, inner), F32),
        ],
        input_output_aliases={} if first else {10: 0},
        name="conv_backward",
    )(order, lengths, pg, xg, branch, branch, x, cw, cb, xw, cb if first else held)


def partner(value, step):
    peers = lax.axis_size("seq")
    return lax.ppermute(value, "seq", [(i, i ^ step) for i in range(peers)])


def halvings():
    step = lax.axis_size("seq") // 2
    while step >= 1:
        yield step
        step //= 2


def reversed_bits(value, peers):
    out = value * 0
    step = 1
    while step < peers:
        out = out * 2 + (value // step) % 2
        step *= 2
    return out


def finish_piece(value):
    for step in reversed(list(halvings())[:-1]):
        half = value.shape[0] // 2
        value = value[:half].astype(F32) + partner(value[half:], step).astype(F32)
        value = value if step == lax.axis_size("seq") // 2 else value.astype(BF16)
    return value


def sum_over_pieces(value):
    for step in reversed(list(halvings())[:-1]):
        value = value.astype(F32) + partner(value, step).astype(F32)
        value = value if step == lax.axis_size("seq") // 2 else value.astype(BF16)
    return value


def sum_to_owner(whole):
    ranks = lax.axis_size("dp")
    me = lax.axis_index("dp")
    share = whole.shape[1] // ranks
    parts = jnp.stack([lax.dynamic_slice_in_dim(whole, (me ^ r) * share, share, 1) for r in range(ranks)]).astype(F32)
    step = 1
    while parts.shape[0] > 1:
        parts = parts.reshape((parts.shape[0] // 2, 2) + parts.shape[1:])
        given = parts[:, 1].astype(BF16)
        other = lax.ppermute(given, "dp", [(i, i ^ step) for i in range(ranks)])
        parts = parts[:, 0] + other.astype(F32)
        step *= 2
    return parts[0]


def dot(left, right, dims, kind=F32):
    return lax.dot_general(left, right, (dims, ((), ())), preferred_element_type=kind)


def body(tokens, lengths, cotangent, norm_gain, in_weight, conv_weight, conv_bias, x_weight, dt_weight,
         dt_bias, a_log, skip_d, out_weight):
    micros, slots, piece, width = tokens.shape
    peers, groups = lax.axis_size("seq"), lax.axis_size("dp")
    me = lax.axis_index("seq")
    share = conv_bias.shape[0]
    inner = share * groups
    rows = in_weight.shape[0]
    rank = dt_weight.shape[0]
    states = a_log.shape[0]
    cols = x_weight.shape[1]
    length = piece * peers
    order = reversed_bits(jnp.arange(peers, dtype=jnp.int32) ^ me, peers)
    tokens, cotangent = tokens[:, 0], cotangent[:, 0]
    held = lengths[:, 0]

    gain_part = norm_gain
    for step in halvings():
        gain_part = jnp.concatenate([gain_part, partner(gain_part, step)])
    gain_part = gain_part.reshape(peers, rows)
    gain_part = jnp.concatenate([lax.dynamic_slice_in_dim(gain_part, order[q], 1) for q in range(peers)])
    gain_rows = peers * rows // share
    small = jnp.concatenate([
        a_log, conv_weight, conv_bias[None], dt_bias[None], skip_d[None], gain_part.reshape(gain_rows, share),
        jnp.zeros((states - KCONV - 3 - gain_rows, share), BF16), dt_weight, x_weight.T], axis=0)
    packed = small.shape[0]

    def mine(half):
        own = half.reshape(rows, groups, peers, share).transpose(2, 0, 1, 3).reshape(peers * rows, inner)
        return lax.all_to_all(own, "seq", split_axis=0, concat_axis=0, tiled=True)

    first = jnp.concatenate([mine(in_weight[:, :inner * peers]), small.reshape(-1, inner)], axis=0)
    first = lax.all_gather(first, "dp", axis=0, tiled=False)
    pieces = [[tokens[m]] for m in range(micros)]
    for step in halvings():
        for m in range(micros):
            pieces[m] = pieces[m] + [partner(part, step) for part in pieces[m]]
    late, pieces = lax.optimization_barrier((in_weight[:, inner * peers:], pieces))
    wg = lax.all_gather(mine(late), "dp", axis=0, tiled=True)
    wo = lax.all_gather(out_weight, "dp", axis=0, tiled=True)
    wb = first[:, :peers * rows].reshape(width, inner)
    small = first[:, peers * rows:].reshape(groups, packed, share)
    at = states + KCONV + 3
    gain = small[:, at:at + gain_rows].reshape(1, width).astype(F32)
    small = jnp.concatenate([small[d] for d in range(groups)], axis=1)
    alog = small[0:states]
    at = states
    cw = small[at:at + KCONV].astype(F32)
    cb = small[at + KCONV:at + KCONV + 1].astype(F32)
    dtb = small[at + KCONV + 1:at + KCONV + 2].astype(F32)
    skip = small[at + KCONV + 2:at + KCONV + 3].astype(F32)
    dtw = small[2 * states:2 * states + rank]
    xw = small[2 * states + rank:]

    positions = me * piece + jnp.arange(piece, dtype=jnp.int32)
    valid = (positions[None, :] < lengths).astype(F32)[..., None]
    own_grad = (valid * cotangent.astype(F32)).astype(BF16)
    own_grad, pieces = lax.optimization_barrier((own_grad, pieces))
    grads = [own_grad]
    for step in list(halvings())[:-1]:
        grads = grads + [partner(part, step) for part in grads]
    convs, normed = [], None
    for m in range(micros):
        normed, branch, x, proj = conv_forward(order, held, pieces[m], gain, wb, cw, cb, xw, rank, m, micros, normed)
        proj = (proj + partner(proj, 1)).astype(BF16)
        if m + 1 < micros:
            proj, pieces[m + 1], grads = lax.optimization_barrier((proj, pieces[m + 1], grads))
        convs.append((branch, x, sum_over_pieces(proj)))
    grads = grads + [partner(part, 1) for part in grads]
    y, starts = None, []
    for m in range(micros):
        y, start = scan_forward(order, held, convs[m][2], convs[m][1], dtw, dtb, alog, skip, m, micros, y)
        starts.append(start)
    normed, y = lax.optimization_barrier((normed, y))
    gate = dot(normed, wg, ((1,), (0,)))
    sig = jax.nn.sigmoid(gate)
    yf = y.astype(F32)
    gated = (yf * gate * sig).astype(BF16)
    out_grad = jnp.concatenate(grads, axis=0).reshape(micros * length, width)
    gwo = dot(gated, out_grad, ((0,), (0,)), BF16)
    gwo, gated, out_grad = lax.optimization_barrier((gwo, gated, out_grad))
    gg = dot(out_grad, wo, ((1,), (1,)))
    sg = (gg * gate * sig).astype(BF16)
    gate_grad = (gg * yf * sig * (1.0 + gate * (1.0 - sig))).astype(BF16)
    half = micros * length // 2
    given = dot(gated[half:], wo, ((1,), (0,)), BF16)
    kept = dot(gated[:half], wo, ((1,), (0,)), BF16)
    given, kept, gate_grad = lax.optimization_barrier((given, kept, gate_grad))
    gwg = dot(normed, gate_grad, ((0,), (0,)), BF16)
    added = (kept.astype(F32) + partner(given, 1).astype(F32)).astype(BF16)
    gwg, sg, added = lax.optimization_barrier((gwg, sg, added))
    added = finish_piece(added)
    gwo = lax.psum_scatter(gwo, "dp", scatter_dimension=0, tiled=True)
    gwg = lax.psum_scatter(gwg, "dp", scatter_dimension=0, tiled=True)
    gwg = lax.all_to_all(gwg, "seq", split_axis=0, concat_axis=0, tiled=True)
    backs = []
    for m in range(micros):
        given = sg
        if m == micros - 1:
            given, gwo, added = lax.optimization_barrier((given, gwo, added))
            result = (valid * (tokens.astype(F32) + added.reshape(micros, piece, width))).astype(BF16)
        backs.append(list(scan_backward(
            order, held, convs[m][2], convs[m][1], given, starts[m], dtw, dtb, alog, skip, m, micros)))
        backs[m][0] = (backs[m][0] + partner(backs[m][0], 1)).astype(BF16)
        if m + 1 < micros:
            backs[m][0] = sum_over_pieces(backs[m][0])
    for m in range(micros - 1):
        backs[m][0], backs[-1][1] = lax.optimization_barrier((backs[m][0], backs[-1][1]))
    mixed, totals = None, None
    for m in range(micros):
        pg, xg, gdtw, gdtb, galog, gskip = backs[m]
        if m == micros - 1:
            pg, mixed, gate_grad = lax.optimization_barrier((pg, mixed, gate_grad))
            pg = sum_over_pieces(pg)
            early = dot(gate_grad, wg, ((1,), (1,)))
            pg, early = lax.optimization_barrier((pg, early))
        mixed, gxw, gcb, gcw = conv_backward(
            order, held, pg, xg, convs[m][0], convs[m][1], cw, cb, xw, m, micros, mixed)
        part = [galog, gcw, gcb, gdtb, gskip, gdtw, gxw]
        totals = part if totals is None else [a + b for a, b in zip(totals, part)]
    gwb = dot(normed, mixed, ((0,), (0,)), BF16)
    gwb, totals, mixed = lax.optimization_barrier((gwb, totals, mixed))
    gwb = lax.psum_scatter(gwb, "dp", scatter_dimension=0, tiled=True)
    gsmall = sum_to_owner(jnp.concatenate(totals, axis=0))
    w = (early + dot(mixed, wb, ((1,), (1,)))).astype(BF16)
    w = finish_piece((w[:half].astype(F32) + partner(w[half:], 1).astype(F32)).astype(BF16)).reshape(micros, piece, width)
    w, gwb, gsmall, gwg = lax.optimization_barrier((w, gwb, gsmall, gwg))
    w = w * gain
    inputs = tokens.astype(F32)
    scale = lax.rsqrt(jnp.mean(inputs * inputs, axis=-1, keepdims=True) + EPSILON)
    input_grad = (own_grad.astype(F32) + scale * w - inputs * (scale * scale * scale)
                  * jnp.mean(w * inputs, axis=-1, keepdims=True)).astype(BF16)
    gwb = lax.all_to_all(gwb, "seq", split_axis=0, concat_axis=0, tiled=True)
    spread = lambda g: g.astype(F32).reshape(peers, rows, groups, share).transpose(1, 2, 0, 3).reshape(rows, inner * peers)
    total = jnp.concatenate([spread(gwb), spread(gwg)], axis=1)
    g_gain = jnp.sum(in_weight.astype(F32) * total, axis=1) / norm_gain.astype(F32)
    pieces, at = [], 0
    for count in (states, KCONV, 1, 1, 1, rank, cols):
        pieces.append(gsmall[at:at + count])
        at += count
    galog, gcw, gcb, gdtb, gskip, gdtw, gxw = pieces
    return (
        result[:, None], input_grad[:, None], g_gain, total, gcw, gcb[0], gxw.T, gdtw, gdtb[0], galog, gskip[0],
        gwo.astype(F32),
    )


def solution(mesh):
    placed = (
        P(None, "dp", "seq", None),
        P(None, "dp"),
        P(None, "dp", "seq", None),
        P(("dp", "seq")),
        P(("dp", "seq"), None),
        P(None, ("dp", "seq")),
        P(("dp", "seq")),
        P(("dp", "seq"), None),
        P(None, ("dp", "seq")),
        P(("dp", "seq")),
        P(None, ("dp", "seq")),
        P(("dp", "seq")),
        P(("dp", "seq"), None),
    )
    return jax.shard_map(
        body,
        mesh=mesh,
        in_specs=placed,
        out_specs=(
            P(None, "dp", "seq", None),
            P(None, "dp", "seq", None),
            P(("dp", "seq")),
            P(("dp", "seq"), None),
            P(None, ("dp", "seq")),
            P(("dp", "seq")),
            P(("dp", "seq"), None),
            P(None, ("dp", "seq")),
            P(("dp", "seq")),
            P(None, ("dp", "seq")),
            P(("dp", "seq")),
            P(("dp", "seq"), None),
        ),
        check_vma=False,
    )
```
